32 devices in a mesh: grp: 2 (over y), ctx: 4 (over z), head: 4 (over x, core).
Axes of the slice: x: 2, y: 2, z: 4, core: 2. Of those that a mesh axis runs over, the one named last changes fastest.
Arguments:
- queries: bfloat16 [1024, 8192], P(('grp', 'ctx'), 'head'), parts along dimension 0, may hold values from -5 to 5
- keys: bfloat16 [1024, 1024], P(('grp', 'ctx'), 'head'), parts along dimension 0, may hold values from -5 to 5
- values: bfloat16 [1024, 1024], P(('grp', 'ctx'), 'head'), parts along dimension 0, may hold values from -6 to 6
- d_out: bfloat16 [1024, 8192], P(('grp', 'ctx'), 'head'), parts along dimension 0, may hold values from -6 to 6
- span_order: int32 [4], replicated, may hold values from 0 to 3, each once
- pattern: int32 [4, 2], replicated, may hold values from 0 to 3, as said below
Outputs:
- d_queries: bfloat16 [1024, 8192], P(('grp', 'ctx'), 'head'), parts along dimension 0
- key_gradients: bfloat16 [1024, 1024], P(('grp', 'ctx'), 'head'), parts along dimension 0
- value_gradients: bfloat16 [1024, 1024], P(('grp', 'ctx'), 'head'), parts along dimension 0
The draws below stay inside these ranges and needn't reach their ends.
There are 2 independent parts, one for each index of `grp`. The reference program is written for one: setup_inputs(seed, part) draws one part's arguments, and reference() takes and returns one part's arrays. A program takes and returns all parts, laid end to end along the dimension named above; an argument that names none is the same for every part. Nothing has to cross between parts.
Inputs may be any that keep to these rules, and one draw needn't show every extreme that they name: `span_order`: a permutation of the 4 block positions. `pattern`: each row names 2 distinct blocks, its own block first.
All inputs are finite; a program needn't handle non-finite values.
Results may differ from the reference program's by a relative error of at most 0.0075.
Values may be sent and summed in bfloat16 or wider, within the bound.
No kernel may reach another device: no remote copies, remote signals or barrier semaphores. Data moves between devices by JAX's collectives and lax.ppermute only.
A program may use at most 64 MiB of HBM per device.

```python
import math
import jax
import jax.numpy as jnp
from jax import lax

QUERY_HEADS = 64
KEY_VALUE_HEADS = 8
HEAD_SIZE = 128
BLOCK = 128
PROMPT_TOKENS = 512
NBLK = 4
NSEL = 2


def draw_queries(key, part):
    final_result = jnp.clip(jax.random.normal(jax.random.fold_in(key, 1), (PROMPT_TOKENS, QUERY_HEADS * HEAD_SIZE), jnp.float32), -5.0, 5.0)
    return final_result.astype(jnp.bfloat16)


def draw_keys(key, part):
    final_result = jnp.clip(jax.random.normal(jax.random.fold_in(key, 2), (PROMPT_TOKENS, KEY_VALUE_HEADS * HEAD_SIZE), jnp.float32), -5.0, 5.0)
    return final_result.astype(jnp.bfloat16)


def draw_pattern(key, part):
    raw = jax.random.randint(jax.random.fold_in(key, 5), (NBLK, NBLK), 0, 2 ** 20)
    column_index = jnp.arange(NBLK, dtype=jnp.int32)
    scores = raw * NBLK + column_index[None, :]
    scores = jnp.where(column_index[:, None] == column_index[None, :], -1, scores)
    order = jnp.argsort(scores, axis=1, stable=True)
    return order[:, :NSEL].astype(jnp.int32)


def levels(own_key, dims, cuts, least, largest):
    factor_of, own = 1.0, jax.random.fold_in(own_key, 6)
    for axis_at, parts in cuts:
        heights = jnp.exp(jax.random.uniform(jax.random.fold_in(own, axis_at), (parts,), jnp.float32, least / len(cuts), largest / len(cuts)))
        factor_of = factor_of * jnp.repeat(heights, dims[axis_at] // parts).reshape([-1 if axis == axis_at else 1 for axis in range(len(dims))])
    return factor_of


def bell_draw(stream_key, extent, spread, reach, shards=(), kind=jnp.bfloat16):
    factor_of = levels(stream_key, extent, shards, -0.22, 0.18) if shards else 1.0
    values = jax.random.normal(stream_key, extent, jnp.float32) * spread * factor_of
    return jnp.minimum(jnp.maximum(values, -reach), reach).astype(kind)


def setup_inputs(seed: int = 0, part: int = 0) -> dict:
    key_of = jax.random.split(jax.random.key(seed), 7)
    part_keys = jax.random.split(jax.random.fold_in(key_of[6], part), 7)
    queries = draw_queries(jax.random.fold_in(jax.random.fold_in(key_of[6], part), 71), part)
    keys = draw_keys(jax.random.fold_in(jax.random.fold_in(key_of[6], part), 71), part)
    values = bell_draw(part_keys[2], (PROMPT_TOKENS, KEY_VALUE_HEADS * HEAD_SIZE), 1.0, 6.0, ((0, 4), (1, 4)))
    d_out = bell_draw(part_keys[3], (PROMPT_TOKENS, QUERY_HEADS * HEAD_SIZE), 1.0, 6.0, ((0, 4), (1, 4)))
    span_order = jax.random.permutation(key_of[4], NBLK).astype(jnp.int32)
    pattern = draw_pattern(jax.random.fold_in(key_of[6], 71), part)
    return {"queries": queries, "keys": keys, "values": values, "d_out": d_out, "span_order": span_order, "pattern": pattern}


NEG = -1e+30

def reference(queries, keys, values, d_out, span_order, pattern):
    query_group = QUERY_HEADS // KEY_VALUE_HEADS
    scale = 1.0 / math.sqrt(HEAD_SIZE)
    tok = jnp.arange(PROMPT_TOKENS, dtype=jnp.int32)
    pos = span_order[tok // BLOCK] * BLOCK + tok % BLOCK
    named = jnp.any(pattern[:, :, None] == jnp.arange(NBLK, dtype=jnp.int32)[None, None, :], axis=1)
    named = jnp.repeat(jnp.repeat(named, BLOCK, axis=0), BLOCK, axis=1)
    allowed = named & (pos[None, :] <= pos[:, None])

    def one_head(head):
        kv_head = head // query_group
        query_h = lax.dynamic_slice_in_dim(queries, head * HEAD_SIZE, HEAD_SIZE, 1)
        grad_h = lax.dynamic_slice_in_dim(d_out, head * HEAD_SIZE, HEAD_SIZE, 1)
        key_h = lax.dynamic_slice_in_dim(keys, kv_head * HEAD_SIZE, HEAD_SIZE, 1)
        value_h = lax.dynamic_slice_in_dim(values, kv_head * HEAD_SIZE, HEAD_SIZE, 1)
        scores = jnp.dot(query_h, key_h.T, preferred_element_type=jnp.float32) * scale
        row_max = lax.optimization_barrier(jnp.max(jnp.where(allowed, scores, NEG), axis=1))
        total = lax.optimization_barrier(jnp.sum(jnp.where(allowed, jnp.exp(scores - row_max[:, None]), 0.0), axis=1))
        lse = row_max + jnp.log(total)
        probs = jnp.where(allowed, jnp.exp(scores - lse[:, None]), 0.0)
        attended = jnp.dot(probs, value_h.astype(jnp.float32), precision=lax.Precision.HIGHEST)
        delta = lax.optimization_barrier(jnp.sum(grad_h.astype(jnp.float32) * attended, axis=1))
        d_probs = jnp.dot(grad_h, value_h.T, preferred_element_type=jnp.float32)
        d_scores = (probs * (d_probs - delta[:, None])).astype(jnp.bfloat16)
        probs_low = probs.astype(jnp.bfloat16)
        d_query = jnp.dot(d_scores, key_h, preferred_element_type=jnp.float32) * scale
        d_key = jnp.dot(d_scores.T, query_h, preferred_element_type=jnp.float32) * scale
        d_value = jnp.dot(probs_low.T, grad_h, preferred_element_type=jnp.float32)
        return (d_query, d_key, d_value)
    d_query_all, key_gradient_total, value_gradient_total = lax.map(one_head, jnp.arange(QUERY_HEADS, dtype=jnp.int32))
    d_queries = d_query_all.transpose(1, 0, 2).reshape(PROMPT_TOKENS, QUERY_HEADS * HEAD_SIZE).astype(jnp.bfloat16)
    key_gradients = key_gradient_total.reshape(KEY_VALUE_HEADS, query_group, PROMPT_TOKENS, HEAD_SIZE).sum(axis=1)
    value_gradients = value_gradient_total.reshape(KEY_VALUE_HEADS, query_group, PROMPT_TOKENS, HEAD_SIZE).sum(axis=1)
    key_gradients = key_gradients.transpose(1, 0, 2).reshape(PROMPT_TOKENS, KEY_VALUE_HEADS * HEAD_SIZE).astype(jnp.bfloat16)
    value_gradients = value_gradients.transpose(1, 0, 2).reshape(PROMPT_TOKENS, KEY_VALUE_HEADS * HEAD_SIZE).astype(jnp.bfloat16)
    return (d_queries, key_gradients, value_gradients)
```

```python
import functools
import itertools
import math

import jax
import jax.numpy as jnp
import numpy as np
from jax import lax
from jax.experimental import pallas as pl
from jax.experimental.pallas import tpu as pltpu
from jax.sharding import PartitionSpec as P

QUERY_HEADS = 64
KEY_VALUE_HEADS = 8
HEAD_SIZE = 128
BLOCK = 128


NEG = -1e30


def routes(count):
    table, sets = np.zeros(count**count, np.int32), []
    for digits in itertools.product(range(count), repeat=count):
        source = [(i + c) % count if c else None for i, c in enumerate(digits)]

        def ends(i):
            for _ in range(count):
                if i is None:
                    return True
                i = source[i]
            return i is None

        if not all(ends(i) for i in range(count)):
            continue
        rounds = []
        for target, origin in enumerate(source):
            if origin is None:
                continue
            for pairs in rounds:
                if all(origin != o for o, _ in pairs):
                    pairs.append((origin, target))
                    break
            else:
                rounds.append([(origin, target)])
        table[sum(c * count**i for i, c in enumerate(digits))] = len(sets)
        sets.append(rounds)
    return sets, table


def prepare_kernel(count, order_ref, pattern_ref, table_ref, keys_ref, values_ref, joined_ref, route_ref):
    code = jnp.int32(0)
    for i in range(count):
        other = pattern_ref[i, 1]
        shift = other - i
        shift = jnp.where(shift < 0, shift + count, shift)
        code += jnp.where(order_ref[other] < order_ref[i], shift, 0) * count**i
    route_ref[0] = table_ref[code]
    width = keys_ref.shape[1]
    joined_ref[:, :width] = keys_ref[...]
    joined_ref[:, width:] = values_ref[...]


def main_kernel(
    query_group,
    order_ref,
    pattern_ref,
    block_ref,
    queries_ref,
    grads_ref,
    own_ref,
    other_ref,
    d_queries_ref,
    own_grads_ref,
    other_grads_ref,
):
    rows = queries_ref.shape[0]
    width = own_ref.shape[1] // 2
    scale = 1.0 / math.sqrt(HEAD_SIZE)
    block = block_ref[0]
    needed = order_ref[pattern_ref[block, 1]] < order_ref[block]
    key_index = lax.broadcasted_iota(jnp.int32, (2 * rows, rows), 0)
    query_index = lax.broadcasted_iota(jnp.int32, (2 * rows, rows), 1)
    limit = jnp.where(needed, 2 * rows, 0)
    allowed = (key_index <= query_index) | ((key_index >= rows) & (key_index < limit))
    for group in range(width // HEAD_SIZE):
        columns = slice(group * HEAD_SIZE, (group + 1) * HEAD_SIZE)
        value_columns = slice(width + group * HEAD_SIZE, width + (group + 1) * HEAD_SIZE)
        key = jnp.concatenate((own_ref[:, columns], other_ref[:, columns]), axis=0)
        value = jnp.concatenate((own_ref[:, value_columns], other_ref[:, value_columns]), axis=0)
        key_total = jnp.zeros((2 * rows, HEAD_SIZE), jnp.float32)
        value_total = jnp.zeros((2 * rows, HEAD_SIZE), jnp.float32)
        for head in range(group * query_group, (group + 1) * query_group):
            head_columns = slice(head * HEAD_SIZE, (head + 1) * HEAD_SIZE)
            query = queries_ref[:, head_columns]
            grad = grads_ref[:, head_columns]
            scores = lax.dot_general(
                key, query, (((1,), (1,)), ((), ())), preferred_element_type=jnp.float32
            )
            scores = jnp.where(allowed, scores * scale, NEG)
            top = jnp.max(scores, axis=0, keepdims=True)
            probs = jnp.exp(scores - top)
            probs = probs * (1.0 / jnp.sum(probs, axis=0, keepdims=True))
            d_probs = lax.dot_general(
                value, grad, (((1,), (1,)), ((), ())), preferred_element_type=jnp.float32
            )
            delta = jnp.sum(probs * d_probs, axis=0, keepdims=True)
            d_scores = (probs * (d_probs - delta)).astype(jnp.bfloat16)
            key_total += jnp.dot(d_scores, query, preferred_element_type=jnp.float32)
            value_total += jnp.dot(
                probs.astype(jnp.bfloat16), grad, preferred_element_type=jnp.float32
            )
            d_query = lax.dot_general(
                d_scores, key, (((0,), (0,)), ((), ())), preferred_element_type=jnp.float32
            )
            d_queries_ref[:, head_columns] = (d_query * scale).astype(jnp.bfloat16)
        key_total = key_total * scale
        own_grads_ref[:, columns] = key_total[:rows]
        own_grads_ref[:, value_columns] = value_total[:rows]
        other_grads_ref[:, columns] = key_total[rows:].astype(jnp.bfloat16)
        other_grads_ref[:, value_columns] = value_total[rows:].astype(jnp.bfloat16)


def routed(queries, keys, values, d_out, span_order, pattern):
    rows, width = keys.shape
    count = pattern.shape[0]
    smem = pl.BlockSpec(memory_space=pltpu.SMEM)
    vmem = pl.BlockSpec(memory_space=pltpu.VMEM)
    sets, table = routes(count)
    joined, route = pl.pallas_call(
        functools.partial(prepare_kernel, count),
        out_shape=(
            jax.ShapeDtypeStruct((rows, 2 * width), jnp.bfloat16),
            jax.ShapeDtypeStruct((1,), jnp.int32),
        ),
        in_specs=[smem, smem, smem, vmem, vmem],
        out_specs=(vmem, smem),
        name="prepare",
    )(span_order, pattern, jnp.asarray(table), keys, values)

    def fetch(rounds):
        def branch(joined):
            parts = [lax.ppermute(joined, "ctx", pairs) for pairs in rounds]
            return functools.reduce(jnp.add, parts) if parts else jnp.zeros_like(joined)

        return branch

    other = lax.switch(route[0], [fetch(rounds) for rounds in sets], joined)
    block = lax.axis_index("ctx").astype(jnp.int32).reshape(1)
    d_queries, own_grads, other_grads = pl.pallas_call(
        functools.partial(main_kernel, QUERY_HEADS // KEY_VALUE_HEADS),
        out_shape=(
            jax.ShapeDtypeStruct(queries.shape, jnp.bfloat16),
            jax.ShapeDtypeStruct((rows, 2 * width), jnp.float32),
            jax.ShapeDtypeStruct((rows, 2 * width), jnp.bfloat16),
        ),
        in_specs=[smem, smem, smem, vmem, vmem, vmem, vmem],
        out_specs=(vmem, vmem, vmem),
        name="attend",
    )(span_order, pattern, block, queries, d_out, joined, other)

    def give_back(rounds):
        def branch(own_grads, other_grads):
            for pairs in rounds:
                back = [(target, source) for source, target in pairs]
                own_grads = own_grads + lax.ppermute(other_grads, "ctx", back).astype(jnp.float32)
            return (
                own_grads[:, :width].astype(jnp.bfloat16),
                own_grads[:, width:].astype(jnp.bfloat16),
            )

        return branch

    key_gradients, value_gradients = lax.switch(
        route[0], [give_back(rounds) for rounds in sets], own_grads, other_grads
    )
    return (d_queries, key_gradients, value_gradients)


def heads_first(dense_matrix, key_value_count):
    return dense_matrix.reshape(
        dense_matrix.shape[0], key_value_count, QUERY_HEADS // KEY_VALUE_HEADS, HEAD_SIZE
    ).transpose(1, 2, 0, 3)


def key_mask(start, count, local_pattern, query_pos, span_order):
    key_blocks = start // BLOCK + jnp.arange(count // BLOCK, dtype=jnp.int32)
    named = jnp.any(local_pattern[:, :, None] == key_blocks[None, None, :], axis=1)
    local_blocks = local_pattern.shape[0]
    named_rows = jnp.broadcast_to(
        named[:, None, :, None], (local_blocks, BLOCK, count // BLOCK, BLOCK)
    )
    named_rows = named_rows.reshape(local_blocks * BLOCK, count)
    key_order = lax.dynamic_slice_in_dim(span_order, start // BLOCK, count // BLOCK, 0)
    key_pos = (key_order[:, None] * BLOCK + jnp.arange(BLOCK, dtype=jnp.int32)[None, :]).reshape(
        count
    )
    return named_rows & (key_pos[None, :] <= query_pos[:, None])


def sweep(step, carry, key_piece, value_piece, start):
    count = key_piece.shape[0]
    width = BLOCK * math.gcd(count // BLOCK, max(1, 512 // BLOCK))
    turns = count // width
    if turns == 1:
        return step(carry, key_piece, value_piece, start)

    def advance(index, inner):
        offset = index * width
        key_part = lax.dynamic_slice_in_dim(key_piece, offset, width, 0)
        value_part = lax.dynamic_slice_in_dim(value_piece, offset, width, 0)
        return step(inner, key_part, value_part, start + offset)

    return lax.fori_loop(0, turns, advance, carry)


def swept(queries, keys, values, d_out, span_order, pattern):
    rows = queries.shape[0]
    key_value_count = keys.shape[1] // HEAD_SIZE
    query_group = QUERY_HEADS // KEY_VALUE_HEADS
    blocks_here = rows // BLOCK
    scale = 1.0 / math.sqrt(HEAD_SIZE)
    first_block = lax.axis_index("ctx") * blocks_here
    local_pattern = lax.dynamic_slice_in_dim(pattern, first_block, blocks_here, 0)
    local_order = lax.dynamic_slice_in_dim(span_order, first_block, blocks_here, 0)
    query_pos = (
        local_order[:, None] * BLOCK + jnp.arange(BLOCK, dtype=jnp.int32)[None, :]
    ).reshape(rows)
    query_heads = heads_first(queries, key_value_count)
    grad_heads = heads_first(d_out, key_value_count)
    total_rows = rows * lax.axis_size("ctx")

    def scores_for(key_piece):
        key_heads = key_piece.reshape(key_piece.shape[0], key_value_count, HEAD_SIZE)
        return (
            jnp.einsum("kgtd,rkd->kgtr", query_heads, key_heads, preferred_element_type=jnp.float32)
            * scale
        )

    def forward_step(carry, key_piece, value_piece, start):
        allowed = key_mask(start, key_piece.shape[0], local_pattern, query_pos, span_order)

        def forward_update(state):
            running_max, total, weighted = state
            scores = scores_for(key_piece)
            new_max = jnp.maximum(running_max, jnp.max(jnp.where(allowed, scores, NEG), axis=-1))
            factor = jnp.exp(running_max - new_max)
            weights = jnp.where(allowed, jnp.exp(scores - new_max[..., None]), 0.0)
            value_heads = value_piece.reshape(
                value_piece.shape[0], key_value_count, HEAD_SIZE
            ).astype(jnp.float32)
            product = jnp.einsum(
                "kgtr,rkd->kgtd", weights, value_heads, precision=lax.Precision.HIGHEST
            )
            return (
                new_max,
                total * factor + jnp.sum(weights, axis=-1),
                weighted * factor[..., None] + product,
            )

        return lax.cond(jnp.any(allowed), forward_update, lambda state: state, carry)

    def make_backward(log_total, delta, anchor):

        def step(carry, key_piece, value_piece, start):
            count = key_piece.shape[0]
            allowed = key_mask(start, count, local_pattern, query_pos, span_order)

            def step_update(state):
                query_grad, key_grads = state
                key_heads = key_piece.reshape(count, key_value_count, HEAD_SIZE)
                value_heads = value_piece.reshape(count, key_value_count, HEAD_SIZE)
                scores = scores_for(key_piece)
                probs = jnp.where(allowed, jnp.exp(scores - log_total[..., None]), 0.0)
                grad_probs = jnp.einsum(
                    "kgtd,rkd->kgtr", grad_heads, value_heads, preferred_element_type=jnp.float32
                )
                grad_scores = (probs * (grad_probs - delta[..., None])).astype(jnp.bfloat16)
                query_grad = query_grad + jnp.einsum(
                    "kgtr,rkd->kgtd", grad_scores, key_heads, preferred_element_type=jnp.float32
                )
                key_part = (
                    jnp.einsum(
                        "kgtr,kgtd->rkd",
                        grad_scores,
                        query_heads,
                        preferred_element_type=jnp.float32,
                    )
                    * scale
                )
                value_part = jnp.einsum(
                    "kgtr,kgtd->rkd",
                    probs.astype(jnp.bfloat16),
                    grad_heads,
                    preferred_element_type=jnp.float32,
                )
                joined = jnp.stack(
                    (
                        key_part.reshape(count, key_value_count * HEAD_SIZE),
                        value_part.reshape(count, key_value_count * HEAD_SIZE),
                    ),
                    axis=1,
                )
                offset = start - anchor
                former = lax.dynamic_slice_in_dim(key_grads, offset, count, 0)
                key_grads = lax.dynamic_update_slice_in_dim(key_grads, former + joined, offset, 0)
                return (query_grad, key_grads)

            return lax.cond(jnp.any(allowed), step_update, lambda state: state, carry)

        return step

    start_state = (
        jnp.full((key_value_count, query_group, rows), NEG, jnp.float32),
        jnp.zeros((key_value_count, query_group, rows), jnp.float32),
        jnp.zeros((key_value_count, query_group, rows, HEAD_SIZE), jnp.float32),
    )
    query_zero = jnp.zeros((key_value_count, query_group, rows, HEAD_SIZE), jnp.float32)
    state = sweep(
        forward_step,
        start_state,
        lax.all_gather(keys, "ctx", axis=0, tiled=True),
        lax.all_gather(values, "ctx", axis=0, tiled=True),
        jnp.int32(0),
    )
    running_max, total, weighted = state
    attended = weighted / total[..., None]
    log_total = running_max + jnp.log(total)
    delta = jnp.sum(grad_heads * attended, axis=-1)
    log_total, delta = (log_total, delta)
    both_step = make_backward(log_total, delta, 0)
    grad_zero = jnp.zeros((total_rows, 2, key_value_count * HEAD_SIZE), jnp.float32)
    query_grad, key_grads = sweep(
        both_step,
        (query_zero, grad_zero),
        lax.all_gather(keys, "ctx", axis=0, tiled=True),
        lax.all_gather(values, "ctx", axis=0, tiled=True),
        jnp.int32(0),
    )
    summed = lax.psum_scatter(key_grads, "ctx", scatter_dimension=0, tiled=True)
    d_queries = (
        (query_grad * scale)
        .transpose(2, 0, 1, 3)
        .reshape(rows, key_value_count * query_group * HEAD_SIZE)
        .astype(jnp.bfloat16)
    )
    key_gradients = summed[:, 0, :].astype(jnp.bfloat16)
    value_gradients = summed[:, 1, :].astype(jnp.bfloat16)
    return (d_queries, key_gradients, value_gradients)


def on_device(queries, keys, values, d_out, span_order, pattern):
    count = lax.axis_size("ctx")
    if count <= 4 and keys.shape[0] == BLOCK and pattern.shape == (count, 2):
        return routed(queries, keys, values, d_out, span_order, pattern)
    return swept(queries, keys, values, d_out, span_order, pattern)


def solution(mesh):
    return jax.shard_map(
        on_device,
        mesh=mesh,
        in_specs=(
            P(("grp", "ctx"), "head"),
            P(("grp", "ctx"), "head"),
            P(("grp", "ctx"), "head"),
            P(("grp", "ctx"), "head"),
            P(),
            P(),
        ),
        out_specs=(P(("grp", "ctx"), "head"), P(("grp", "ctx"), "head"), P(("grp", "ctx"), "head")),
        check_vma=False,
    )
```

```python
import functools
import itertools
import math

import jax
import jax.numpy as jnp
import numpy as np
from jax import lax
from jax.experimental import pallas as pl
from jax.experimental.pallas import tpu as pltpu
from jax.sharding import PartitionSpec as P

QUERY_HEADS = 64
KEY_VALUE_HEADS = 8
HEAD_SIZE = 128
BLOCK = 128


NEG = -1e30


def routes(count):
    def load(rounds):
        links = np.zeros((2, count), np.int32)
        for source, target in itertools.chain(*rounds):
            links[int(source < target), min(source, target) : max(source, target)] += 1
        return links.max()

    cycles = []
    for rest in itertools.permutations(range(1, count)):
        order = (0, *rest)
        cycles.append([(order[k], order[(k + 1) % count]) for k in range(count)])
    candidates = []
    for rounds in range(1, 4):
        for chosen in itertools.combinations(cycles, rounds):
            taken, distinct = set(), []
            for cycle in chosen:
                distinct.append([pair for pair in cycle if pair not in taken])
                taken.update(cycle)
            if all(distinct):
                candidates.append((rounds, load(distinct), taken, distinct))
    candidates.sort(key=lambda candidate: candidate[:2])
    table, chosen = np.zeros(count**count, np.int32), []
    for shifts in itertools.product(range(count), repeat=count):
        need = {((i + shift) % count, i) for i, shift in enumerate(shifts) if shift}
        last = {i for i in range(count) if not shifts[i]}
        for _ in range(count):
            last |= {target for source, target in need if source in last}
        if len(last) < count:
            continue
        fit = [k for k, candidate in enumerate(candidates) if need <= candidate[2]]
        if fit[0] not in chosen:
            chosen.append(fit[0])
        table[sum(shift * count**i for i, shift in enumerate(shifts))] = chosen.index(fit[0])
    sets = [candidates[k][3] for k in chosen]
    sources = np.full((len(sets), 3, count), -1, np.int32)
    targets = np.full((len(sets), 3, count), -1, np.int32)
    for k, rounds in enumerate(sets):
        for r, pairs in enumerate(rounds):
            for source, target in pairs:
                sources[k, r, target], targets[k, r, source] = source, target
    return sets, np.concatenate((table, sources.ravel(), targets.ravel()))


def prepare_kernel(count, routes_count, order_ref, pattern_ref, table_ref, keys_ref, values_ref, joined_ref, plan_ref):
    code = jnp.int32(0)
    for i in range(count):
        other = pattern_ref[1, i]
        shift = jnp.where(other < i, other - i + count, other - i)
        code += jnp.where(order_ref[other] < order_ref[i], shift, 0) * count**i
    route = table_ref[code]
    block = lax.axis_index("ctx")
    mine = pattern_ref[1, block]
    plan_ref[0] = route
    take = jnp.int32(0)
    for r in range(3):
        place = count**count + (route * 3 + r) * count + block
        take = jnp.where(table_ref[place] == mine, r, take)
        reader = table_ref[place + routes_count * 3 * count]
        at = jnp.maximum(reader, 0)
        wanted = (reader >= 0) & (pattern_ref[1, at] == block)
        plan_ref[2 + r] = wanted.astype(jnp.int32)
    plan_ref[1] = take
    plan_ref[5] = (order_ref[mine] < order_ref[block]).astype(jnp.int32)
    width = keys_ref.shape[1]
    joined_ref[:, :width] = keys_ref[...]
    joined_ref[:, width:] = values_ref[...]


def main_kernel(
    query_group,
    plan_ref,
    queries_ref,
    grads_ref,
    own_ref,
    other_ref,
    d_queries_ref,
    own_grads_ref,
    other_grads_ref,
):
    rows = queries_ref.shape[0]
    width = own_ref.shape[1] // 2
    scale = 1.0 / math.sqrt(HEAD_SIZE)
    key_index = lax.broadcasted_iota(jnp.int32, (2 * rows, rows), 0)
    query_index = lax.broadcasted_iota(jnp.int32, (2 * rows, rows), 1)
    limit = plan_ref[5] * 2 * rows
    allowed = (key_index <= query_index) | ((key_index >= rows) & (key_index < limit))
    for group in range(width // HEAD_SIZE):
        columns = slice(group * HEAD_SIZE, (group + 1) * HEAD_SIZE)
        value_columns = slice(width + group * HEAD_SIZE, width + (group + 1) * HEAD_SIZE)
        key = jnp.concatenate((own_ref[:, columns], other_ref[:, columns]), axis=0)
        value = jnp.concatenate((own_ref[:, value_columns], other_ref[:, value_columns]), axis=0)
        key_total = jnp.zeros((2 * rows, HEAD_SIZE), jnp.float32)
        value_total = jnp.zeros((2 * rows, HEAD_SIZE), jnp.float32)
        for head in range(group * query_group, (group + 1) * query_group):
            head_columns = slice(head * HEAD_SIZE, (head + 1) * HEAD_SIZE)
            query = queries_ref[:, head_columns]
            grad = grads_ref[:, head_columns]
            scores = lax.dot_general(
                key, query, (((1,), (1,)), ((), ())), preferred_element_type=jnp.float32
            )
            scores = jnp.where(allowed, scores * scale, NEG)
            top = jnp.max(scores, axis=0, keepdims=True)
            probs = jnp.exp(scores - top)
            probs = probs * (1.0 / jnp.sum(probs, axis=0, keepdims=True))
            d_probs = lax.dot_general(
                value, grad, (((1,), (1,)), ((), ())), preferred_element_type=jnp.float32
            )
            delta = jnp.sum(probs * d_probs, axis=0, keepdims=True)
            d_scores = (probs * (d_probs - delta)).astype(jnp.bfloat16)
            key_total += jnp.dot(d_scores, query, preferred_element_type=jnp.float32)
            value_total += jnp.dot(
                probs.astype(jnp.bfloat16), grad, preferred_element_type=jnp.float32
            )
            d_query = lax.dot_general(
                d_scores, key, (((0,), (0,)), ((), ())), preferred_element_type=jnp.float32
            )
            d_queries_ref[:, head_columns] = (d_query * scale).astype(jnp.bfloat16)
        key_total = key_total * scale
        own_grads_ref[:, columns] = key_total[:rows]
        own_grads_ref[:, value_columns] = value_total[:rows]
        other_grads_ref[:, columns] = key_total[rows:].astype(jnp.bfloat16)
        other_grads_ref[:, value_columns] = value_total[rows:].astype(jnp.bfloat16)


def routed(queries, keys, values, d_out, span_order, pattern):
    rows, width = keys.shape
    count = pattern.shape[0]
    smem = pl.BlockSpec(memory_space=pltpu.SMEM)
    vmem = pl.BlockSpec(memory_space=pltpu.VMEM)
    sets, table = routes(count)
    joined, plan = pl.pallas_call(
        functools.partial(prepare_kernel, count, len(sets)),
        out_shape=(
            jax.ShapeDtypeStruct((rows, 2 * width), jnp.bfloat16),
            jax.ShapeDtypeStruct((6,), jnp.int32),
        ),
        in_specs=[smem, smem, smem, vmem, vmem],
        out_specs=(vmem, smem),
        name="prepare",
    )(span_order, pattern.T, jnp.asarray(table), keys, values)

    def fetch(rounds):
        def branch(plan, joined):
            parts = [lax.ppermute(joined, "ctx", pairs) for pairs in rounds]
            other = parts[0]
            for r in range(1, len(parts)):
                other = jnp.where(plan[1] == r, parts[r], other)
            return other

        return branch

    other = lax.switch(plan[0], [fetch(rounds) for rounds in sets], plan, joined)
    d_queries, own_grads, other_grads = pl.pallas_call(
        functools.partial(main_kernel, QUERY_HEADS // KEY_VALUE_HEADS),
        out_shape=(
            jax.ShapeDtypeStruct(queries.shape, jnp.bfloat16),
            jax.ShapeDtypeStruct((rows, 2 * width), jnp.float32),
            jax.ShapeDtypeStruct((rows, 2 * width), jnp.bfloat16),
        ),
        in_specs=[smem, vmem, vmem, vmem, vmem],
        out_specs=(vmem, vmem, vmem),
        name="attend",
    )(plan, queries, d_out, joined, other)

    def give_back(rounds):
        def branch(plan, own_grads, other_grads):
            for r, pairs in enumerate(rounds):
                back = [(target, source) for source, target in pairs]
                part = lax.ppermute(other_grads, "ctx", back).astype(jnp.float32)
                own_grads = own_grads + jnp.where(plan[2 + r] > 0, part, 0.0)
            return (
                own_grads[:, :width].astype(jnp.bfloat16),
                own_grads[:, width:].astype(jnp.bfloat16),
            )

        return branch

    key_gradients, value_gradients = lax.switch(
        plan[0], [give_back(rounds) for rounds in sets], plan, own_grads, other_grads
    )
    return (d_queries, key_gradients, value_gradients)


def heads_first(dense_matrix, key_value_count):
    return dense_matrix.reshape(
        dense_matrix.shape[0], key_value_count, QUERY_HEADS // KEY_VALUE_HEADS, HEAD_SIZE
    ).transpose(1, 2, 0, 3)


def key_mask(start, count, local_pattern, query_pos, span_order):
    key_blocks = start // BLOCK + jnp.arange(count // BLOCK, dtype=jnp.int32)
    named = jnp.any(local_pattern[:, :, None] == key_blocks[None, None, :], axis=1)
    local_blocks = local_pattern.shape[0]
    named_rows = jnp.broadcast_to(
        named[:, None, :, None], (local_blocks, BLOCK, count // BLOCK, BLOCK)
    )
    named_rows = named_rows.reshape(local_blocks * BLOCK, count)
    key_order = lax.dynamic_slice_in_dim(span_order, start // BLOCK, count // BLOCK, 0)
    key_pos = (key_order[:, None] * BLOCK + jnp.arange(BLOCK, dtype=jnp.int32)[None, :]).reshape(
        count
    )
    return named_rows & (key_pos[None, :] <= query_pos[:, None])


def sweep(step, carry, key_piece, value_piece, start):
    count = key_piece.shape[0]
    width = BLOCK * math.gcd(count // BLOCK, max(1, 512 // BLOCK))
    turns = count // width
    if turns == 1:
        return step(carry, key_piece, value_piece, start)

    def advance(index, inner):
        offset = index * width
        key_part = lax.dynamic_slice_in_dim(key_piece, offset, width, 0)
        value_part = lax.dynamic_slice_in_dim(value_piece, offset, width, 0)
        return step(inner, key_part, value_part, start + offset)

    return lax.fori_loop(0, turns, advance, carry)


def swept(queries, keys, values, d_out, span_order, pattern):
    rows = queries.shape[0]
    key_value_count = keys.shape[1] // HEAD_SIZE
    query_group = QUERY_HEADS // KEY_VALUE_HEADS
    blocks_here = rows // BLOCK
    scale = 1.0 / math.sqrt(HEAD_SIZE)
    first_block = lax.axis_index("ctx") * blocks_here
    local_pattern = lax.dynamic_slice_in_dim(pattern, first_block, blocks_here, 0)
    local_order = lax.dynamic_slice_in_dim(span_order, first_block, blocks_here, 0)
    query_pos = (
        local_order[:, None] * BLOCK + jnp.arange(BLOCK, dtype=jnp.int32)[None, :]
    ).reshape(rows)
    query_heads = heads_first(queries, key_value_count)
    grad_heads = heads_first(d_out, key_value_count)
    total_rows = rows * lax.axis_size("ctx")

    def scores_for(key_piece):
        key_heads = key_piece.reshape(key_piece.shape[0], key_value_count, HEAD_SIZE)
        return (
            jnp.einsum("kgtd,rkd->kgtr", query_heads, key_heads, preferred_element_type=jnp.float32)
            * scale
        )

    def forward_step(carry, key_piece, value_piece, start):
        allowed = key_mask(start, key_piece.shape[0], local_pattern, query_pos, span_order)

        def forward_update(state):
            running_max, total, weighted = state
            scores = scores_for(key_piece)
            new_max = jnp.maximum(running_max, jnp.max(jnp.where(allowed, scores, NEG), axis=-1))
            factor = jnp.exp(running_max - new_max)
            weights = jnp.where(allowed, jnp.exp(scores - new_max[..., None]), 0.0)
            value_heads = value_piece.reshape(
                value_piece.shape[0], key_value_count, HEAD_SIZE
            ).astype(jnp.float32)
            product = jnp.einsum(
                "kgtr,rkd->kgtd", weights, value_heads, precision=lax.Precision.HIGHEST
            )
            return (
                new_max,
                total * factor + jnp.sum(weights, axis=-1),
                weighted * factor[..., None] + product,
            )

        return lax.cond(jnp.any(allowed), forward_update, lambda state: state, carry)

    def make_backward(log_total, delta, anchor):

        def step(carry, key_piece, value_piece, start):
            count = key_piece.shape[0]
            allowed = key_mask(start, count, local_pattern, query_pos, span_order)

            def step_update(state):
                query_grad, key_grads = state
                key_heads = key_piece.reshape(count, key_value_count, HEAD_SIZE)
                value_heads = value_piece.reshape(count, key_value_count, HEAD_SIZE)
                scores = scores_for(key_piece)
                probs = jnp.where(allowed, jnp.exp(scores - log_total[..., None]), 0.0)
                grad_probs = jnp.einsum(
                    "kgtd,rkd->kgtr", grad_heads, value_heads, preferred_element_type=jnp.float32
                )
                grad_scores = (probs * (grad_probs - delta[..., None])).astype(jnp.bfloat16)
                query_grad = query_grad + jnp.einsum(
                    "kgtr,rkd->kgtd", grad_scores, key_heads, preferred_element_type=jnp.float32
                )
                key_part = (
                    jnp.einsum(
                        "kgtr,kgtd->rkd",
                        grad_scores,
                        query_heads,
                        preferred_element_type=jnp.float32,
                    )
                    * scale
                )
                value_part = jnp.einsum(
                    "kgtr,kgtd->rkd",
                    probs.astype(jnp.bfloat16),
                    grad_heads,
                    preferred_element_type=jnp.float32,
                )
                joined = jnp.stack(
                    (
                        key_part.reshape(count, key_value_count * HEAD_SIZE),
                        value_part.reshape(count, key_value_count * HEAD_SIZE),
                    ),
                    axis=1,
                )
                offset = start - anchor
                former = lax.dynamic_slice_in_dim(key_grads, offset, count, 0)
                key_grads = lax.dynamic_update_slice_in_dim(key_grads, former + joined, offset, 0)
                return (query_grad, key_grads)

            return lax.cond(jnp.any(allowed), step_update, lambda state: state, carry)

        return step

    start_state = (
        jnp.full((key_value_count, query_group, rows), NEG, jnp.float32),
        jnp.zeros((key_value_count, query_group, rows), jnp.float32),
        jnp.zeros((key_value_count, query_group, rows, HEAD_SIZE), jnp.float32),
    )
    query_zero = jnp.zeros((key_value_count, query_group, rows, HEAD_SIZE), jnp.float32)
    state = sweep(
        forward_step,
        start_state,
        lax.all_gather(keys, "ctx", axis=0, tiled=True),
        lax.all_gather(values, "ctx", axis=0, tiled=True),
        jnp.int32(0),
    )
    running_max, total, weighted = state
    attended = weighted / total[..., None]
    log_total = running_max + jnp.log(total)
    delta = jnp.sum(grad_heads * attended, axis=-1)
    log_total, delta = (log_total, delta)
    both_step = make_backward(log_total, delta, 0)
    grad_zero = jnp.zeros((total_rows, 2, key_value_count * HEAD_SIZE), jnp.float32)
    query_grad, key_grads = sweep(
        both_step,
        (query_zero, grad_zero),
        lax.all_gather(keys, "ctx", axis=0, tiled=True),
        lax.all_gather(values, "ctx", axis=0, tiled=True),
        jnp.int32(0),
    )
    summed = lax.psum_scatter(key_grads, "ctx", scatter_dimension=0, tiled=True)
    d_queries = (
        (query_grad * scale)
        .transpose(2, 0, 1, 3)
        .reshape(rows, key_value_count * query_group * HEAD_SIZE)
        .astype(jnp.bfloat16)
    )
    key_gradients = summed[:, 0, :].astype(jnp.bfloat16)
    value_gradients = summed[:, 1, :].astype(jnp.bfloat16)
    return (d_queries, key_gradients, value_gradients)


def on_device(queries, keys, values, d_out, span_order, pattern):
    count = lax.axis_size("ctx")
    if count <= 4 and keys.shape[0] == BLOCK and pattern.shape == (count, 2):
        return routed(queries, keys, values, d_out, span_order, pattern)
    return swept(queries, keys, values, d_out, span_order, pattern)


def solution(mesh):
    return jax.shard_map(
        on_device,
        mesh=mesh,
        in_specs=(
            P(("grp", "ctx"), "head"),
            P(("grp", "ctx"), "head"),
            P(("grp", "ctx"), "head"),
            P(("grp", "ctx"), "head"),
            P(),
            P(),
        ),
        out_specs=(P(("grp", "ctx"), "head"), P(("grp", "ctx"), "head"), P(("grp", "ctx"), "head")),
        check_vma=False,
    )
```

```python
import functools
import itertools
import math

import jax
import jax.numpy as jnp
import numpy as np
from jax import lax
from jax.experimental import pallas as pl
from jax.experimental.pallas import tpu as pltpu
from jax.sharding import PartitionSpec as P

QUERY_HEADS = 64
KEY_VALUE_HEADS = 8
HEAD_SIZE = 128
BLOCK = 128


NEG = -1e30


def routes(count):
    def load(rounds):
        links = np.zeros((2, count), np.int32)
        for source, target in itertools.chain(*rounds):
            links[int(source < target), min(source, target) : max(source, target)] += 1
        return links.max()

    cycles = []
    for rest in itertools.permutations(range(1, count)):
        order = (0, *rest)
        cycles.append([(order[k], order[(k + 1) % count]) for k in range(count)])
    candidates = []
    for rounds in range(1, 4):
        for chosen in itertools.combinations(cycles, rounds):
            taken, distinct = set(), []
            for cycle in chosen:
                distinct.append([pair for pair in cycle if pair not in taken])
                taken.update(cycle)
            if all(distinct):
                candidates.append((rounds, load(distinct), taken, distinct))
    candidates.sort(key=lambda candidate: candidate[:2])
    table, chosen = np.zeros(count**count, np.int32), []
    for shifts in itertools.product(range(count), repeat=count):
        need = {((i + shift) % count, i) for i, shift in enumerate(shifts) if shift}
        last = {i for i in range(count) if not shifts[i]}
        for _ in range(count):
            last |= {target for source, target in need if source in last}
        if len(last) < count:
            continue
        fit = [k for k, candidate in enumerate(candidates) if need <= candidate[2]]
        if fit[0] not in chosen:
            chosen.append(fit[0])
        table[sum(shift * count**i for i, shift in enumerate(shifts))] = chosen.index(fit[0])
    sets = [candidates[k][3] for k in chosen]
    sources = np.full((len(sets), 3, count), -1, np.int32)
    targets = np.full((len(sets), 3, count), -1, np.int32)
    for k, rounds in enumerate(sets):
        for r, pairs in enumerate(rounds):
            for source, target in pairs:
                sources[k, r, target], targets[k, r, source] = source, target
    return sets, np.concatenate((table, sources.ravel(), targets.ravel()))


def prepare_kernel(count, routes_count, order_ref, pattern_ref, table_ref, keys_ref, values_ref, joined_ref, plan_ref):
    code = jnp.int32(0)
    for i in range(count):
        other = pattern_ref[1, i]
        shift = jnp.where(other < i, other - i + count, other - i)
        code += jnp.where(order_ref[other] < order_ref[i], shift, 0) * count**i
    route = table_ref[code]
    block = lax.axis_index("ctx")
    mine = pattern_ref[1, block]
    plan_ref[0] = route
    take = jnp.int32(0)
    for r in range(3):
        place = count**count + (route * 3 + r) * count + block
        take = jnp.where(table_ref[place] == mine, r, take)
        reader = table_ref[place + routes_count * 3 * count]
        at = jnp.maximum(reader, 0)
        wanted = (reader >= 0) & (pattern_ref[1, at] == block)
        plan_ref[2 + r] = wanted.astype(jnp.int32)
    plan_ref[1] = take
    plan_ref[5] = (order_ref[mine] < order_ref[block]).astype(jnp.int32)
    width = keys_ref.shape[1]
    joined_ref[:, :width] = keys_ref[...]
    joined_ref[:, width:] = values_ref[...]


def main_kernel(
    query_group,
    plan_ref,
    queries_ref,
    grads_ref,
    own_ref,
    other_ref,
    d_queries_ref,
    own_grads_ref,
    other_grads_ref,
):
    rows = queries_ref.shape[0]
    width = own_ref.shape[1] // 2
    scale = 1.0 / math.sqrt(HEAD_SIZE)
    shape = (2 * rows, query_group * rows)
    key_index = lax.broadcasted_iota(jnp.int32, shape, 0)
    query_index = lax.broadcasted_iota(jnp.int32, shape, 1) % rows
    limit = plan_ref[5] * 2 * rows
    allowed = (key_index <= query_index) | ((key_index >= rows) & (key_index < limit))
    bias = jnp.where(allowed, 0.0, NEG)
    for group in range(width // HEAD_SIZE):
        columns = slice(group * HEAD_SIZE, (group + 1) * HEAD_SIZE)
        value_columns = slice(width + group * HEAD_SIZE, width + (group + 1) * HEAD_SIZE)
        key = jnp.concatenate((own_ref[:, columns], other_ref[:, columns]), axis=0)
        value = jnp.concatenate((own_ref[:, value_columns], other_ref[:, value_columns]), axis=0)
        heads = [
            slice(head * HEAD_SIZE, (head + 1) * HEAD_SIZE)
            for head in range(group * query_group, (group + 1) * query_group)
        ]
        query = jnp.concatenate([queries_ref[:, head] for head in heads], axis=0)
        grad = jnp.concatenate([grads_ref[:, head] for head in heads], axis=0)
        scores = lax.dot_general(
            key, query, (((1,), (1,)), ((), ())), preferred_element_type=jnp.float32
        )
        scores = scores * (scale * math.log2(math.e)) + bias
        probs = jnp.exp2(scores - jnp.max(scores, axis=0, keepdims=True))
        probs = probs * (1.0 / jnp.sum(probs, axis=0, keepdims=True))
        d_probs = lax.dot_general(
            value, grad, (((1,), (1,)), ((), ())), preferred_element_type=jnp.float32
        )
        delta = jnp.sum(probs * d_probs, axis=0, keepdims=True)
        d_scores = (probs * (d_probs - delta)).astype(jnp.bfloat16)
        d_key = jnp.dot(d_scores, query, preferred_element_type=jnp.float32) * scale
        d_value = jnp.dot(probs.astype(jnp.bfloat16), grad, preferred_element_type=jnp.float32)
        d_query = lax.dot_general(
            d_scores, key, (((0,), (0,)), ((), ())), preferred_element_type=jnp.float32
        )
        d_query = (d_query * scale).astype(jnp.bfloat16)
        for index, head in enumerate(heads):
            d_queries_ref[:, head] = d_query[index * rows : (index + 1) * rows]
        own_grads_ref[:, columns] = d_key[:rows]
        own_grads_ref[:, value_columns] = d_value[:rows]
        other_grads_ref[:, columns] = d_key[rows:].astype(jnp.bfloat16)
        other_grads_ref[:, value_columns] = d_value[rows:].astype(jnp.bfloat16)


def routed(queries, keys, values, d_out, span_order, pattern):
    rows, width = keys.shape
    count = pattern.shape[0]
    smem = pl.BlockSpec(memory_space=pltpu.SMEM)
    vmem = pl.BlockSpec(memory_space=pltpu.VMEM)
    sets, table = routes(count)
    joined, plan = pl.pallas_call(
        functools.partial(prepare_kernel, count, len(sets)),
        out_shape=(
            jax.ShapeDtypeStruct((rows, 2 * width), jnp.bfloat16),
            jax.ShapeDtypeStruct((6,), jnp.int32),
        ),
        in_specs=[smem, smem, smem, vmem, vmem],
        out_specs=(vmem, smem),
        name="prepare",
    )(span_order, pattern.T, jnp.asarray(table), keys, values)

    def fetch(rounds):
        def branch(plan, joined):
            parts = [lax.ppermute(joined, "ctx", pairs) for pairs in rounds]
            other = parts[0]
            for r in range(1, len(parts)):
                other = jnp.where(plan[1] == r, parts[r], other)
            return other

        return branch

    other = lax.switch(plan[0], [fetch(rounds) for rounds in sets], plan, joined)
    d_queries, own_grads, other_grads = pl.pallas_call(
        functools.partial(main_kernel, QUERY_HEADS // KEY_VALUE_HEADS),
        out_shape=(
            jax.ShapeDtypeStruct(queries.shape, jnp.bfloat16),
            jax.ShapeDtypeStruct((rows, 2 * width), jnp.float32),
            jax.ShapeDtypeStruct((rows, 2 * width), jnp.bfloat16),
        ),
        in_specs=[smem, vmem, vmem, vmem, vmem],
        out_specs=(vmem, vmem, vmem),
        compiler_params=pltpu.CompilerParams(vmem_limit_bytes=16 << 20),
        name="attend",
    )(plan, queries, d_out, joined, other)

    def give_back(rounds):
        def branch(plan, own_grads, other_grads):
            for r, pairs in enumerate(rounds):
                back = [(target, source) for source, target in pairs]
                part = lax.ppermute(other_grads, "ctx", back).astype(jnp.float32)
                own_grads = own_grads + jnp.where(plan[2 + r] > 0, part, 0.0)
            return (
                own_grads[:, :width].astype(jnp.bfloat16),
                own_grads[:, width:].astype(jnp.bfloat16),
            )

        return branch

    key_gradients, value_gradients = lax.switch(
        plan[0], [give_back(rounds) for rounds in sets], plan, own_grads, other_grads
    )
    return (d_queries, key_gradients, value_gradients)


def heads_first(dense_matrix, key_value_count):
    return dense_matrix.reshape(
        dense_matrix.shape[0], key_value_count, QUERY_HEADS // KEY_VALUE_HEADS, HEAD_SIZE
    ).transpose(1, 2, 0, 3)


def key_mask(start, count, local_pattern, query_pos, span_order):
    key_blocks = start // BLOCK + jnp.arange(count // BLOCK, dtype=jnp.int32)
    named = jnp.any(local_pattern[:, :, None] == key_blocks[None, None, :], axis=1)
    local_blocks = local_pattern.shape[0]
    named_rows = jnp.broadcast_to(
        named[:, None, :, None], (local_blocks, BLOCK, count // BLOCK, BLOCK)
    )
    named_rows = named_rows.reshape(local_blocks * BLOCK, count)
    key_order = lax.dynamic_slice_in_dim(span_order, start // BLOCK, count // BLOCK, 0)
    key_pos = (key_order[:, None] * BLOCK + jnp.arange(BLOCK, dtype=jnp.int32)[None, :]).reshape(
        count
    )
    return named_rows & (key_pos[None, :] <= query_pos[:, None])


def sweep(step, carry, key_piece, value_piece, start):
    count = key_piece.shape[0]
    width = BLOCK * math.gcd(count // BLOCK, max(1, 512 // BLOCK))
    turns = count // width
    if turns == 1:
        return step(carry, key_piece, value_piece, start)

    def advance(index, inner):
        offset = index * width
        key_part = lax.dynamic_slice_in_dim(key_piece, offset, width, 0)
        value_part = lax.dynamic_slice_in_dim(value_piece, offset, width, 0)
        return step(inner, key_part, value_part, start + offset)

    return lax.fori_loop(0, turns, advance, carry)


def swept(queries, keys, values, d_out, span_order, pattern):
    rows = queries.shape[0]
    key_value_count = keys.shape[1] // HEAD_SIZE
    query_group = QUERY_HEADS // KEY_VALUE_HEADS
    blocks_here = rows // BLOCK
    scale = 1.0 / math.sqrt(HEAD_SIZE)
    first_block = lax.axis_index("ctx") * blocks_here
    local_pattern = lax.dynamic_slice_in_dim(pattern, first_block, blocks_here, 0)
    local_order = lax.dynamic_slice_in_dim(span_order, first_block, blocks_here, 0)
    query_pos = (
        local_order[:, None] * BLOCK + jnp.arange(BLOCK, dtype=jnp.int32)[None, :]
    ).reshape(rows)
    query_heads = heads_first(queries, key_value_count)
    grad_heads = heads_first(d_out, key_value_count)
    total_rows = rows * lax.axis_size("ctx")

    def scores_for(key_piece):
        key_heads = key_piece.reshape(key_piece.shape[0], key_value_count, HEAD_SIZE)
        return (
            jnp.einsum("kgtd,rkd->kgtr", query_heads, key_heads, preferred_element_type=jnp.float32)
            * scale
        )

    def forward_step(carry, key_piece, value_piece, start):
        allowed = key_mask(start, key_piece.shape[0], local_pattern, query_pos, span_order)

        def forward_update(state):
            running_max, total, weighted = state
            scores = scores_for(key_piece)
            new_max = jnp.maximum(running_max, jnp.max(jnp.where(allowed, scores, NEG), axis=-1))
            factor = jnp.exp(running_max - new_max)
            weights = jnp.where(allowed, jnp.exp(scores - new_max[..., None]), 0.0)
            value_heads = value_piece.reshape(
                value_piece.shape[0], key_value_count, HEAD_SIZE
            ).astype(jnp.float32)
            product = jnp.einsum(
                "kgtr,rkd->kgtd", weights, value_heads, precision=lax.Precision.HIGHEST
            )
            return (
                new_max,
                total * factor + jnp.sum(weights, axis=-1),
                weighted * factor[..., None] + product,
            )

        return lax.cond(jnp.any(allowed), forward_update, lambda state: state, carry)

    def make_backward(log_total, delta, anchor):

        def step(carry, key_piece, value_piece, start):
            count = key_piece.shape[0]
            allowed = key_mask(start, count, local_pattern, query_pos, span_order)

            def step_update(state):
                query_grad, key_grads = state
                key_heads = key_piece.reshape(count, key_value_count, HEAD_SIZE)
                value_heads = value_piece.reshape(count, key_value_count, HEAD_SIZE)
                scores = scores_for(key_piece)
                probs = jnp.where(allowed, jnp.exp(scores - log_total[..., None]), 0.0)
                grad_probs = jnp.einsum(
                    "kgtd,rkd->kgtr", grad_heads, value_heads, preferred_element_type=jnp.float32
                )
                grad_scores = (probs * (grad_probs - delta[..., None])).astype(jnp.bfloat16)
                query_grad = query_grad + jnp.einsum(
                    "kgtr,rkd->kgtd", grad_scores, key_heads, preferred_element_type=jnp.float32
                )
                key_part = (
                    jnp.einsum(
                        "kgtr,kgtd->rkd",
                        grad_scores,
                        query_heads,
                        preferred_element_type=jnp.float32,
                    )
                    * scale
                )
                value_part = jnp.einsum(
                    "kgtr,kgtd->rkd",
                    probs.astype(jnp.bfloat16),
                    grad_heads,
                    preferred_element_type=jnp.float32,
                )
                joined = jnp.stack(
                    (
                        key_part.reshape(count, key_value_count * HEAD_SIZE),
                        value_part.reshape(count, key_value_count * HEAD_SIZE),
                    ),
                    axis=1,
                )
                offset = start - anchor
                former = lax.dynamic_slice_in_dim(key_grads, offset, count, 0)
                key_grads = lax.dynamic_update_slice_in_dim(key_grads, former + joined, offset, 0)
                return (query_grad, key_grads)

            return lax.cond(jnp.any(allowed), step_update, lambda state: state, carry)

        return step

    start_state = (
        jnp.full((key_value_count, query_group, rows), NEG, jnp.float32),
        jnp.zeros((key_value_count, query_group, rows), jnp.float32),
        jnp.zeros((key_value_count, query_group, rows, HEAD_SIZE), jnp.float32),
    )
    query_zero = jnp.zeros((key_value_count, query_group, rows, HEAD_SIZE), jnp.float32)
    state = sweep(
        forward_step,
        start_state,
        lax.all_gather(keys, "ctx", axis=0, tiled=True),
        lax.all_gather(values, "ctx", axis=0, tiled=True),
        jnp.int32(0),
    )
    running_max, total, weighted = state
    attended = weighted / total[..., None]
    log_total = running_max + jnp.log(total)
    delta = jnp.sum(grad_heads * attended, axis=-1)
    log_total, delta = (log_total, delta)
    both_step = make_backward(log_total, delta, 0)
    grad_zero = jnp.zeros((total_rows, 2, key_value_count * HEAD_SIZE), jnp.float32)
    query_grad, key_grads = sweep(
        both_step,
        (query_zero, grad_zero),
        lax.all_gather(keys, "ctx", axis=0, tiled=True),
        lax.all_gather(values, "ctx", axis=0, tiled=True),
        jnp.int32(0),
    )
    summed = lax.psum_scatter(key_grads, "ctx", scatter_dimension=0, tiled=True)
    d_queries = (
        (query_grad * scale)
        .transpose(2, 0, 1, 3)
        .reshape(rows, key_value_count * query_group * HEAD_SIZE)
        .astype(jnp.bfloat16)
    )
    key_gradients = summed[:, 0, :].astype(jnp.bfloat16)
    value_gradients = summed[:, 1, :].astype(jnp.bfloat16)
    return (d_queries, key_gradients, value_gradients)


def on_device(queries, keys, values, d_out, span_order, pattern):
    count = lax.axis_size("ctx")
    if count <= 4 and keys.shape[0] == BLOCK and pattern.shape == (count, 2):
        return routed(queries, keys, values, d_out, span_order, pattern)
    return swept(queries, keys, values, d_out, span_order, pattern)


def solution(mesh):
    return jax.shard_map(
        on_device,
        mesh=mesh,
        in_specs=(
            P(("grp", "ctx"), "head"),
            P(("grp", "ctx"), "head"),
            P(("grp", "ctx"), "head"),
            P(("grp", "ctx"), "head"),
            P(),
            P(),
        ),
        out_specs=(P(("grp", "ctx"), "head"), P(("grp", "ctx"), "head"), P(("grp", "ctx"), "head")),
        check_vma=False,
    )
```

```python
import functools
import itertools
import math

import jax
import jax.numpy as jnp
import numpy as np
from jax import lax
from jax.experimental import pallas as pl
from jax.experimental.pallas import tpu as pltpu
from jax.sharding import PartitionSpec as P

QUERY_HEADS = 64
KEY_VALUE_HEADS = 8
HEAD_SIZE = 128
BLOCK = 128


NEG = -1e30


def routes(count):
    def load(rounds):
        links = np.zeros((2, count), np.int32)
        for source, target in itertools.chain(*rounds):
            links[int(source < target), min(source, target) : max(source, target)] += 1
        return links.max()

    cycles = []
    for rest in itertools.permutations(range(1, count)):
        order = (0, *rest)
        cycles.append([(order[k], order[(k + 1) % count]) for k in range(count)])
    candidates = []
    for rounds in range(1, 3):
        for chosen in itertools.combinations(cycles, rounds):
            taken, distinct = set(), []
            for cycle in chosen:
                distinct.append([pair for pair in cycle if pair not in taken])
                taken.update(cycle)
            if all(distinct):
                candidates.append((rounds, load(distinct), taken, distinct))
    candidates.sort(key=lambda candidate: candidate[:2])
    shifts = [[(i, (i + shift) % count) for i in range(count)] for shift in range(1, count)]
    candidates.append((len(shifts), 0, set(itertools.chain(*shifts)), shifts))
    table, chosen = np.zeros(count**count, np.int32), []
    for shifts in itertools.product(range(count), repeat=count):
        need = {((i + shift) % count, i) for i, shift in enumerate(shifts) if shift}
        last = {i for i in range(count) if not shifts[i]}
        for _ in range(count):
            last |= {target for source, target in need if source in last}
        if len(last) < count:
            continue
        fit = [k for k, candidate in enumerate(candidates) if need <= candidate[2]]
        if fit[0] not in chosen:
            chosen.append(fit[0])
        table[sum(shift * count**i for i, shift in enumerate(shifts))] = chosen.index(fit[0])
    sets = [candidates[k][3] for k in chosen]
    sources = np.full((len(sets), count - 1, count), -1, np.int32)
    targets = np.full((len(sets), count - 1, count), -1, np.int32)
    for k, rounds in enumerate(sets):
        for r, pairs in enumerate(rounds):
            for source, target in pairs:
                sources[k, r, target], targets[k, r, source] = source, target
    return sets, np.concatenate((table, sources.ravel(), targets.ravel()))


def prepare_kernel(count, routes_count, order_ref, pattern_ref, table_ref, keys_ref, values_ref, joined_ref, plan_ref):
    code = jnp.int32(0)
    for i in range(count):
        other = pattern_ref[1, i]
        shift = jnp.where(other < i, other - i + count, other - i)
        code += jnp.where(order_ref[other] < order_ref[i], shift, 0) * count**i
    route = table_ref[code]
    block = lax.axis_index("ctx")
    mine = pattern_ref[1, block]
    plan_ref[0] = route
    take = jnp.int32(0)
    for r in range(count - 1):
        place = count**count + (route * (count - 1) + r) * count + block
        take = jnp.where(table_ref[place] == mine, r, take)
        reader = table_ref[place + routes_count * (count - 1) * count]
        at = jnp.maximum(reader, 0)
        wanted = (reader >= 0) & (pattern_ref[1, at] == block)
        plan_ref[3 + r] = wanted.astype(jnp.int32)
    plan_ref[1] = take
    plan_ref[2] = (order_ref[mine] < order_ref[block]).astype(jnp.int32)
    width = keys_ref.shape[1]
    joined_ref[:, :width] = keys_ref[...]
    joined_ref[:, width:] = values_ref[...]


def columns_of(group, width, query_group):
    start = group * HEAD_SIZE
    heads = [
        slice(head * HEAD_SIZE, (head + 1) * HEAD_SIZE)
        for head in range(group * query_group, (group + 1) * query_group)
    ]
    return slice(start, start + HEAD_SIZE), slice(width + start, width + start + HEAD_SIZE), heads


def stacked(ref, heads):
    return jnp.concatenate([ref[:, head] for head in heads], axis=0)


def against(rows, columns):
    return lax.dot_general(
        rows, columns, (((1,), (1,)), ((), ())), preferred_element_type=jnp.float32
    )


def picked(plan_ref, part_refs):
    other = part_refs[0][...]
    for r in range(1, len(part_refs)):
        other = jnp.where(plan_ref[1] == r, part_refs[r][...], other)
    return other


LOG2_SCALE = math.log2(math.e) / math.sqrt(HEAD_SIZE)
SCALE = 1.0 / math.sqrt(HEAD_SIZE)


def own_kernel(
    query_group,
    queries_ref,
    grads_ref,
    own_ref,
    query_stack_ref,
    grad_stack_ref,
    weights_ref,
    d_probs_ref,
    stats_ref,
):
    rows = queries_ref.shape[0]
    width = own_ref.shape[1] // 2
    shape = (rows, query_group * rows)
    allowed = lax.broadcasted_iota(jnp.int32, shape, 0) <= (
        lax.broadcasted_iota(jnp.int32, shape, 1) % rows
    )
    bias = jnp.where(allowed, 0.0, NEG)
    for group in range(width // HEAD_SIZE):
        key_columns, value_columns, heads = columns_of(group, width, query_group)
        block = slice(group * rows, (group + 1) * rows)
        stack = slice(group * query_group * rows, (group + 1) * query_group * rows)
        query, grad = stacked(queries_ref, heads), stacked(grads_ref, heads)
        query_stack_ref[stack], grad_stack_ref[stack] = query, grad
        scores = against(own_ref[:, key_columns], query) * LOG2_SCALE + bias
        top = jnp.max(scores, axis=0, keepdims=True)
        weights = jnp.exp2(scores - top)
        d_probs = against(own_ref[:, value_columns], grad)
        weights_ref[block] = weights
        d_probs_ref[block] = d_probs
        stats_ref[group * 8 : group * 8 + 1] = top
        stats_ref[group * 8 + 1 : group * 8 + 2] = jnp.sum(weights, axis=0, keepdims=True)
        stats_ref[group * 8 + 2 : group * 8 + 3] = jnp.sum(weights * d_probs, axis=0, keepdims=True)


def other_kernel(
    query_group,
    plan_ref,
    queries_ref,
    grads_ref,
    stats_ref,
    *refs,
):
    *part_refs, sent_ref, d_scores_ref, joint_ref = refs
    other = picked(plan_ref, part_refs)
    rows, width = other.shape[0], other.shape[1] // 2
    bias = jnp.where(plan_ref[2] > 0, 0.0, NEG)
    columns = [columns_of(group, width, query_group)[:2] for group in range(width // HEAD_SIZE)]
    stacks = [
        slice(group * query_group * rows, (group + 1) * query_group * rows)
        for group in range(len(columns))
    ]
    products = [
        (
            against(other[:, key_columns], queries_ref[stack]),
            against(other[:, value_columns], grads_ref[stack]),
        )
        for (key_columns, value_columns), stack in zip(columns, stacks)
    ]
    for group, (scores, d_probs) in enumerate(products):
        key_columns, value_columns = columns[group]
        query, grad = queries_ref[stacks[group]], grads_ref[stacks[group]]
        own_top = stats_ref[group * 8 : group * 8 + 1]
        own_total = stats_ref[group * 8 + 1 : group * 8 + 2]
        own_delta = stats_ref[group * 8 + 2 : group * 8 + 3]
        scores = scores * LOG2_SCALE + bias
        top = jnp.maximum(own_top, jnp.max(scores, axis=0, keepdims=True))
        factor = jnp.exp2(own_top - top)
        weights = jnp.exp2(scores - top)
        inverse = 1.0 / (own_total * factor + jnp.sum(weights, axis=0, keepdims=True))
        delta = (own_delta * factor + jnp.sum(weights * d_probs, axis=0, keepdims=True)) * inverse
        probs = weights * inverse
        d_scores = (probs * (d_probs - delta)).astype(jnp.bfloat16)
        d_scores_ref[group * rows : (group + 1) * rows] = d_scores
        joint_ref[group * 8 : group * 8 + 1] = factor * inverse
        joint_ref[group * 8 + 1 : group * 8 + 2] = delta
        d_key = jnp.dot(d_scores, query, preferred_element_type=jnp.float32) * SCALE
        d_value = jnp.dot(probs.astype(jnp.bfloat16), grad, preferred_element_type=jnp.float32)
        sent_ref[:, key_columns] = d_key.astype(jnp.bfloat16)
        sent_ref[:, value_columns] = d_value.astype(jnp.bfloat16)


def rest_kernel(
    query_group,
    plan_ref,
    queries_ref,
    grads_ref,
    own_ref,
    weights_ref,
    d_probs_ref,
    d_scores_ref,
    joint_ref,
    *refs,
):
    *part_refs, d_queries_ref, own_grads_ref = refs
    other = picked(plan_ref, part_refs)
    rows, width = own_ref.shape[0], own_ref.shape[1] // 2
    for group in range(width // HEAD_SIZE):
        key_columns, value_columns, heads = columns_of(group, width, query_group)
        block = slice(group * rows, (group + 1) * rows)
        stack = slice(group * query_group * rows, (group + 1) * query_group * rows)
        query, grad = queries_ref[stack], grads_ref[stack]
        probs = weights_ref[block] * joint_ref[group * 8 : group * 8 + 1]
        delta = joint_ref[group * 8 + 1 : group * 8 + 2]
        d_scores = (probs * (d_probs_ref[block] - delta)).astype(jnp.bfloat16)
        d_key = jnp.dot(d_scores, query, preferred_element_type=jnp.float32) * SCALE
        d_value = jnp.dot(probs.astype(jnp.bfloat16), grad, preferred_element_type=jnp.float32)
        own_grads_ref[:, key_columns] = d_key
        own_grads_ref[:, value_columns] = d_value
        both = jnp.concatenate((d_scores, d_scores_ref[block]), axis=0)
        key = jnp.concatenate((own_ref[:, key_columns], other[:, key_columns]), axis=0)
        d_query = lax.dot_general(
            both, key, (((0,), (0,)), ((), ())), preferred_element_type=jnp.float32
        )
        d_query = (d_query * SCALE).astype(jnp.bfloat16)
        for index, head in enumerate(heads):
            d_queries_ref[:, head] = d_query[index * rows : (index + 1) * rows]


def routed(queries, keys, values, d_out, span_order, pattern):
    rows, width = keys.shape
    count = pattern.shape[0]
    query_group = QUERY_HEADS // KEY_VALUE_HEADS
    groups = width // HEAD_SIZE
    smem = pl.BlockSpec(memory_space=pltpu.SMEM)
    vmem = pl.BlockSpec(memory_space=pltpu.VMEM)
    sets, table = routes(count)

    def shaped(shape, dtype):
        return jax.ShapeDtypeStruct(shape, dtype)

    def kernel(name, body, results, inputs):
        products = 2 * groups * query_group * rows * rows * HEAD_SIZE
        return pl.pallas_call(
            functools.partial(body, query_group),
            out_shape=results,
            in_specs=[vmem if x.ndim == 2 else smem for x in inputs],
            out_specs=tuple(vmem for _ in results),
            compiler_params=pltpu.CompilerParams(vmem_limit_bytes=16 << 20),
            cost_estimate=pl.CostEstimate(
                flops=4 * products,
                bytes_accessed=sum(x.size * x.dtype.itemsize for x in (*inputs, *results)),
                transcendentals=groups * query_group * rows * rows,
            ),
            name=name,
        )(*inputs)

    wide = (groups * rows, query_group * rows)
    narrow = (groups * 8, query_group * rows)
    stack = shaped((groups * query_group * rows, HEAD_SIZE), jnp.bfloat16)
    joined, plan = pl.pallas_call(
        functools.partial(prepare_kernel, count, len(sets)),
        out_shape=(shaped((rows, 2 * width), jnp.bfloat16), shaped((count + 2,), jnp.int32)),
        in_specs=[smem, smem, smem, vmem, vmem],
        out_specs=(vmem, smem),
        name="prepare",
    )(span_order, pattern.T, jnp.asarray(table), keys, values)

    def along(rounds):
        def branch(plan, queries, d_out, joined):
            parts = [lax.ppermute(joined, "ctx", pairs) for pairs in rounds]
            query_stack, grad_stack, weights, d_probs, stats = kernel(
                "own_block",
                own_kernel,
                (
                    stack,
                    stack,
                    shaped(wide, jnp.float32),
                    shaped(wide, jnp.float32),
                    shaped(narrow, jnp.float32),
                ),
                (queries, d_out, joined),
            )
            sent, d_scores, joint = kernel(
                "other_block",
                other_kernel,
                (
                    shaped((rows, 2 * width), jnp.bfloat16),
                    shaped(wide, jnp.bfloat16),
                    shaped(narrow, jnp.float32),
                ),
                (plan, query_stack, grad_stack, stats, *parts),
            )
            returned = [
                lax.ppermute(sent, "ctx", [(target, source) for source, target in pairs])
                for pairs in rounds
            ]
            d_queries, own_grads = kernel(
                "rest",
                rest_kernel,
                (shaped(queries.shape, jnp.bfloat16), shaped((rows, 2 * width), jnp.float32)),
                (
                    plan,
                    query_stack,
                    grad_stack,
                    joined,
                    weights,
                    d_probs,
                    d_scores,
                    joint,
                    *parts,
                ),
            )
            for r, terms in enumerate(returned):
                terms = terms.astype(jnp.float32)
                if len(returned) > 1:
                    terms = jnp.where(plan[3 + r] > 0, terms, 0.0)
                own_grads = own_grads + terms
            return (
                d_queries,
                own_grads[:, :width].astype(jnp.bfloat16),
                own_grads[:, width:].astype(jnp.bfloat16),
            )

        return branch

    return lax.switch(plan[0], [along(rounds) for rounds in sets], plan, queries, d_out, joined)


def heads_first(dense_matrix, key_value_count):
    return dense_matrix.reshape(
        dense_matrix.shape[0], key_value_count, QUERY_HEADS // KEY_VALUE_HEADS, HEAD_SIZE
    ).transpose(1, 2, 0, 3)


def key_mask(start, count, local_pattern, query_pos, span_order):
    key_blocks = start // BLOCK + jnp.arange(count // BLOCK, dtype=jnp.int32)
    named = jnp.any(local_pattern[:, :, None] == key_blocks[None, None, :], axis=1)
    local_blocks = local_pattern.shape[0]
    named_rows = jnp.broadcast_to(
        named[:, None, :, None], (local_blocks, BLOCK, count // BLOCK, BLOCK)
    )
    named_rows = named_rows.reshape(local_blocks * BLOCK, count)
    key_order = lax.dynamic_slice_in_dim(span_order, start // BLOCK, count // BLOCK, 0)
    key_pos = (key_order[:, None] * BLOCK + jnp.arange(BLOCK, dtype=jnp.int32)[None, :]).reshape(
        count
    )
    return named_rows & (key_pos[None, :] <= query_pos[:, None])


def sweep(step, carry, key_piece, value_piece, start):
    count = key_piece.shape[0]
    width = BLOCK * math.gcd(count // BLOCK, max(1, 512 // BLOCK))
    turns = count // width
    if turns == 1:
        return step(carry, key_piece, value_piece, start)

    def advance(index, inner):
        offset = index * width
        key_part = lax.dynamic_slice_in_dim(key_piece, offset, width, 0)
        value_part = lax.dynamic_slice_in_dim(value_piece, offset, width, 0)
        return step(inner, key_part, value_part, start + offset)

    return lax.fori_loop(0, turns, advance, carry)


def swept(queries, keys, values, d_out, span_order, pattern):
    rows = queries.shape[0]
    key_value_count = keys.shape[1] // HEAD_SIZE
    query_group = QUERY_HEADS // KEY_VALUE_HEADS
    blocks_here = rows // BLOCK
    scale = 1.0 / math.sqrt(HEAD_SIZE)
    first_block = lax.axis_index("ctx") * blocks_here
    local_pattern = lax.dynamic_slice_in_dim(pattern, first_block, blocks_here, 0)
    local_order = lax.dynamic_slice_in_dim(span_order, first_block, blocks_here, 0)
    query_pos = (
        local_order[:, None] * BLOCK + jnp.arange(BLOCK, dtype=jnp.int32)[None, :]
    ).reshape(rows)
    query_heads = heads_first(queries, key_value_count)
    grad_heads = heads_first(d_out, key_value_count)
    total_rows = rows * lax.axis_size("ctx")

    def scores_for(key_piece):
        key_heads = key_piece.reshape(key_piece.shape[0], key_value_count, HEAD_SIZE)
        return (
            jnp.einsum("kgtd,rkd->kgtr", query_heads, key_heads, preferred_element_type=jnp.float32)
            * scale
        )

    def forward_step(carry, key_piece, value_piece, start):
        allowed = key_mask(start, key_piece.shape[0], local_pattern, query_pos, span_order)

        def forward_update(state):
            running_max, total, weighted = state
            scores = scores_for(key_piece)
            new_max = jnp.maximum(running_max, jnp.max(jnp.where(allowed, scores, NEG), axis=-1))
            factor = jnp.exp(running_max - new_max)
            weights = jnp.where(allowed, jnp.exp(scores - new_max[..., None]), 0.0)
            value_heads = value_piece.reshape(
                value_piece.shape[0], key_value_count, HEAD_SIZE
            ).astype(jnp.float32)
            product = jnp.einsum(
                "kgtr,rkd->kgtd", weights, value_heads, precision=lax.Precision.HIGHEST
            )
            return (
                new_max,
                total * factor + jnp.sum(weights, axis=-1),
                weighted * factor[..., None] + product,
            )

        return lax.cond(jnp.any(allowed), forward_update, lambda state: state, carry)

    def make_backward(log_total, delta, anchor):

        def step(carry, key_piece, value_piece, start):
            count = key_piece.shape[0]
            allowed = key_mask(start, count, local_pattern, query_pos, span_order)

            def step_update(state):
                query_grad, key_grads = state
                key_heads = key_piece.reshape(count, key_value_count, HEAD_SIZE)
                value_heads = value_piece.reshape(count, key_value_count, HEAD_SIZE)
                scores = scores_for(key_piece)
                probs = jnp.where(allowed, jnp.exp(scores - log_total[..., None]), 0.0)
                grad_probs = jnp.einsum(
                    "kgtd,rkd->kgtr", grad_heads, value_heads, preferred_element_type=jnp.float32
                )
                grad_scores = (probs * (grad_probs - delta[..., None])).astype(jnp.bfloat16)
                query_grad = query_grad + jnp.einsum(
                    "kgtr,rkd->kgtd", grad_scores, key_heads, preferred_element_type=jnp.float32
                )
                key_part = (
                    jnp.einsum(
                        "kgtr,kgtd->rkd",
                        grad_scores,
                        query_heads,
                        preferred_element_type=jnp.float32,
                    )
                    * scale
                )
                value_part = jnp.einsum(
                    "kgtr,kgtd->rkd",
                    probs.astype(jnp.bfloat16),
                    grad_heads,
                    preferred_element_type=jnp.float32,
                )
                joined = jnp.stack(
                    (
                        key_part.reshape(count, key_value_count * HEAD_SIZE),
                        value_part.reshape(count, key_value_count * HEAD_SIZE),
                    ),
                    axis=1,
                )
                offset = start - anchor
                former = lax.dynamic_slice_in_dim(key_grads, offset, count, 0)
                key_grads = lax.dynamic_update_slice_in_dim(key_grads, former + joined, offset, 0)
                return (query_grad, key_grads)

            return lax.cond(jnp.any(allowed), step_update, lambda state: state, carry)

        return step

    start_state = (
        jnp.full((key_value_count, query_group, rows), NEG, jnp.float32),
        jnp.zeros((key_value_count, query_group, rows), jnp.float32),
        jnp.zeros((key_value_count, query_group, rows, HEAD_SIZE), jnp.float32),
    )
    query_zero = jnp.zeros((key_value_count, query_group, rows, HEAD_SIZE), jnp.float32)
    state = sweep(
        forward_step,
        start_state,
        lax.all_gather(keys, "ctx", axis=0, tiled=True),
        lax.all_gather(values, "ctx", axis=0, tiled=True),
        jnp.int32(0),
    )
    running_max, total, weighted = state
    attended = weighted / total[..., None]
    log_total = running_max + jnp.log(total)
    delta = jnp.sum(grad_heads * attended, axis=-1)
    log_total, delta = (log_total, delta)
    both_step = make_backward(log_total, delta, 0)
    grad_zero = jnp.zeros((total_rows, 2, key_value_count * HEAD_SIZE), jnp.float32)
    query_grad, key_grads = sweep(
        both_step,
        (query_zero, grad_zero),
        lax.all_gather(keys, "ctx", axis=0, tiled=True),
        lax.all_gather(values, "ctx", axis=0, tiled=True),
        jnp.int32(0),
    )
    summed = lax.psum_scatter(key_grads, "ctx", scatter_dimension=0, tiled=True)
    d_queries = (
        (query_grad * scale)
        .transpose(2, 0, 1, 3)
        .reshape(rows, key_value_count * query_group * HEAD_SIZE)
        .astype(jnp.bfloat16)
    )
    key_gradients = summed[:, 0, :].astype(jnp.bfloat16)
    value_gradients = summed[:, 1, :].astype(jnp.bfloat16)
    return (d_queries, key_gradients, value_gradients)


def on_device(queries, keys, values, d_out, span_order, pattern):
    count = lax.axis_size("ctx")
    if count <= 4 and keys.shape[0] == BLOCK and pattern.shape == (count, 2):
        return routed(queries, keys, values, d_out, span_order, pattern)
    return swept(queries, keys, values, d_out, span_order, pattern)


def solution(mesh):
    return jax.shard_map(
        on_device,
        mesh=mesh,
        in_specs=(
            P(("grp", "ctx"), "head"),
            P(("grp", "ctx"), "head"),
            P(("grp", "ctx"), "head"),
            P(("grp", "ctx"), "head"),
            P(),
            P(),
        ),
        out_specs=(P(("grp", "ctx"), "head"), P(("grp", "ctx"), "head"), P(("grp", "ctx"), "head")),
        check_vma=False,
    )
```

```python
import functools
import itertools
import math

import jax
import jax.numpy as jnp
import numpy as np
from jax import lax
from jax.experimental import pallas as pl
from jax.experimental.pallas import tpu as pltpu
from jax.sharding import PartitionSpec as P

QUERY_HEADS = 64
KEY_VALUE_HEADS = 8
HEAD_SIZE = 128
BLOCK = 128


NEG = -1e30


PERMUTATIONS = {
    "a": (1, 2, 3, 0),
    "b": (1, 3, 0, 2),
    "c": (2, 0, 3, 1),
    "d": (3, 0, 1, 2),
    "e": (2, 3, 1, 0),
    "f": (3, 2, 0, 1),
    "s": (1, 0, 3, 2),
    "t": (2, 3, 0, 1),
}
ROUTES = ("s", "b", "c", "a", "d", "e", "f", "ba", "ca", "ts", "bd", "dc", "ad", "adc", "abd")


def route_tables():
    count = 4
    table = np.zeros(count**count, np.int32)
    sources = np.full((len(ROUTES), count - 1, count), -1, np.int32)
    targets = np.full((len(ROUTES), count - 1, count), -1, np.int32)
    pairs = []
    for k, route in enumerate(ROUTES):
        pairs.append(set())
        for r, name in enumerate(route):
            for source, target in enumerate(PERMUTATIONS[name]):
                if (source, target) not in pairs[k]:
                    sources[k, r, target], targets[k, r, source] = source, target
                    pairs[k].add((source, target))
    for shifts in itertools.product(range(count), repeat=count):
        need = {((i + shift) % count, i) for i, shift in enumerate(shifts) if shift}
        last = {i for i in range(count) if not shifts[i]}
        for _ in range(count):
            last |= {target for source, target in need if source in last}
        if len(last) == count:
            code = sum(shift * count**i for i, shift in enumerate(shifts))
            table[code] = next(k for k, held in enumerate(pairs) if need <= held)
    return np.concatenate((table, sources.ravel(), targets.ravel()))


def prepare_kernel(order_ref, pattern_ref, table_ref, keys_ref, values_ref, joined_ref, plan_ref):
    count = pattern_ref.shape[1]
    code = jnp.int32(0)
    for i in range(count):
        other = pattern_ref[1, i]
        shift = jnp.where(other < i, other - i + count, other - i)
        code += jnp.where(order_ref[other] < order_ref[i], shift, 0) * count**i
    route = table_ref[code]
    block = lax.axis_index("ctx")
    mine = pattern_ref[1, block]
    plan_ref[0] = route
    take = jnp.int32(0)
    for r in range(count - 1):
        place = count**count + (route * (count - 1) + r) * count + block
        take = jnp.where(table_ref[place] == mine, r, take)
        reader = table_ref[place + len(ROUTES) * (count - 1) * count]
        at = jnp.maximum(reader, 0)
        wanted = (reader >= 0) & (pattern_ref[1, at] == block)
        plan_ref[3 + r] = wanted.astype(jnp.int32)
    plan_ref[1] = take
    plan_ref[2] = (order_ref[mine] < order_ref[block]).astype(jnp.int32)
    width = keys_ref.shape[1]
    joined_ref[:, :width] = keys_ref[...]
    joined_ref[:, width:] = values_ref[...]


def span(start, size):
    return pl.ds(pl.multiple_of(start, size), size)


def columns_of(group, width, query_group):
    start = group * HEAD_SIZE
    heads = [span((group * query_group + head) * HEAD_SIZE, HEAD_SIZE) for head in range(query_group)]
    return span(start, HEAD_SIZE), span(width + start, HEAD_SIZE), heads


def stacked(ref, heads):
    return jnp.concatenate([ref[:, head] for head in heads], axis=0)


def against(rows, columns):
    return lax.dot_general(
        rows, columns, (((1,), (1,)), ((), ())), preferred_element_type=jnp.float32
    )


def picked(stats_ref, part_refs):
    other = part_refs[0][...]
    if len(part_refs) == 1:
        return other
    taken = jnp.broadcast_to(stats_ref[4:5, : other.shape[1]], other.shape)
    for r in range(1, len(part_refs)):
        other = jnp.where(taken == r, part_refs[r][...], other)
    return other


LOG2_SCALE = math.log2(math.e) / math.sqrt(HEAD_SIZE)
SCALE = 1.0 / math.sqrt(HEAD_SIZE)


def own_kernel(
    query_group,
    plan_ref,
    queries_ref,
    grads_ref,
    own_ref,
    query_stack_ref,
    grad_stack_ref,
    weights_ref,
    d_probs_ref,
    stats_ref,
):
    rule = jnp.where(plan_ref[2] > 0, 0.0, jnp.full((1, stats_ref.shape[1]), NEG))
    turn = jnp.full((1, stats_ref.shape[1]), plan_ref[1].astype(jnp.float32))
    rows = queries_ref.shape[0]
    width = own_ref.shape[1] // 2
    shape = (rows, query_group * rows)
    allowed = lax.broadcasted_iota(jnp.int32, shape, 0) <= (
        lax.broadcasted_iota(jnp.int32, shape, 1) % rows
    )
    bias = jnp.where(allowed, 0.0, NEG)

    @pl.loop(0, width // HEAD_SIZE)
    def _(group):
        key_columns, value_columns, heads = columns_of(group, width, query_group)
        block = span(group * rows, rows)
        stack = span(group * query_group * rows, query_group * rows)
        query, grad = stacked(queries_ref, heads), stacked(grads_ref, heads)
        query_stack_ref[stack], grad_stack_ref[stack] = query, grad
        scores = against(own_ref[:, key_columns], query) * LOG2_SCALE + bias
        top = jnp.max(scores, axis=0, keepdims=True)
        weights = jnp.exp2(scores - top)
        d_probs = against(own_ref[:, value_columns], grad)
        weights_ref[block] = weights
        d_probs_ref[block] = d_probs
        total = jnp.sum(weights, axis=0, keepdims=True)
        delta = jnp.sum(weights * d_probs, axis=0, keepdims=True)
        blank = jnp.zeros((3, top.shape[1]), jnp.float32)
        stats_ref[span(group * 8, 8)] = jnp.concatenate((top, total, delta, rule, turn, blank))


def other_kernel(
    query_group,
    queries_ref,
    grads_ref,
    stats_ref,
    *refs,
):
    *part_refs, sent_ref, d_scores_ref, joint_ref = refs
    other = picked(stats_ref, part_refs)
    rows, width = other.shape[0], other.shape[1] // 2
    bias = stats_ref[3:4]
    columns = [
        (slice(start, start + HEAD_SIZE), slice(width + start, width + start + HEAD_SIZE))
        for start in range(0, width, HEAD_SIZE)
    ]
    stacks = [
        slice(group * query_group * rows, (group + 1) * query_group * rows)
        for group in range(len(columns))
    ]
    products = [
        (
            against(other[:, key_columns], queries_ref[stack]),
            against(other[:, value_columns], grads_ref[stack]),
        )
        for (key_columns, value_columns), stack in zip(columns, stacks)
    ]
    for group, (scores, d_probs) in enumerate(products):
        key_columns, value_columns = columns[group]
        query, grad = queries_ref[stacks[group]], grads_ref[stacks[group]]
        own_top = stats_ref[group * 8 : group * 8 + 1]
        own_total = stats_ref[group * 8 + 1 : group * 8 + 2]
        own_delta = stats_ref[group * 8 + 2 : group * 8 + 3]
        scores = scores * LOG2_SCALE + bias
        top = jnp.maximum(own_top, jnp.max(scores, axis=0, keepdims=True))
        factor = jnp.exp2(own_top - top)
        weights = jnp.exp2(scores - top)
        inverse = 1.0 / (own_total * factor + jnp.sum(weights, axis=0, keepdims=True))
        delta = (own_delta * factor + jnp.sum(weights * d_probs, axis=0, keepdims=True)) * inverse
        probs = weights * inverse
        d_scores = (probs * (d_probs - delta)).astype(jnp.bfloat16)
        d_scores_ref[group * rows : (group + 1) * rows] = d_scores
        joint_ref[group * 8 : group * 8 + 1] = factor * inverse
        joint_ref[group * 8 + 1 : group * 8 + 2] = delta
        d_key = jnp.dot(d_scores, query, preferred_element_type=jnp.float32) * SCALE
        d_value = jnp.dot(probs.astype(jnp.bfloat16), grad, preferred_element_type=jnp.float32)
        sent_ref[:, key_columns] = d_key.astype(jnp.bfloat16)
        sent_ref[:, value_columns] = d_value.astype(jnp.bfloat16)


def rest_kernel(
    query_group,
    queries_ref,
    grads_ref,
    stats_ref,
    own_ref,
    weights_ref,
    d_probs_ref,
    d_scores_ref,
    joint_ref,
    *refs,
):
    *part_refs, d_queries_ref, own_grads_ref, other_keys_ref = refs
    other = picked(stats_ref, part_refs)
    rows, width = own_ref.shape[0], own_ref.shape[1] // 2
    other_keys_ref[...] = other[:, :width]

    @pl.loop(0, width // HEAD_SIZE)
    def _(group):
        key_columns, value_columns, heads = columns_of(group, width, query_group)
        block = span(group * rows, rows)
        stack = span(group * query_group * rows, query_group * rows)
        query, grad = queries_ref[stack], grads_ref[stack]
        joint = joint_ref[span(group * 8, 8)]
        probs = weights_ref[block] * joint[:1]
        d_scores = (probs * (d_probs_ref[block] - joint[1:2])).astype(jnp.bfloat16)
        d_key = jnp.dot(d_scores, query, preferred_element_type=jnp.float32) * SCALE
        d_value = jnp.dot(probs.astype(jnp.bfloat16), grad, preferred_element_type=jnp.float32)
        own_grads_ref[:, key_columns] = d_key
        own_grads_ref[:, value_columns] = d_value
        both = jnp.concatenate((d_scores, d_scores_ref[block]), axis=0)
        key = jnp.concatenate((own_ref[:, key_columns], other_keys_ref[:, key_columns]), axis=0)
        d_query = lax.dot_general(
            both, key, (((0,), (0,)), ((), ())), preferred_element_type=jnp.float32
        )
        d_query = (d_query * SCALE).astype(jnp.bfloat16)
        for index, head in enumerate(heads):
            d_queries_ref[:, head] = d_query[index * rows : (index + 1) * rows]


def routed(queries, keys, values, d_out, span_order, pattern):
    rows, width = keys.shape
    count = pattern.shape[0]
    query_group = QUERY_HEADS // KEY_VALUE_HEADS
    groups = width // HEAD_SIZE
    smem = pl.BlockSpec(memory_space=pltpu.SMEM)
    vmem = pl.BlockSpec(memory_space=pltpu.VMEM)

    def shaped(shape, dtype):
        return jax.ShapeDtypeStruct(shape, dtype)

    def kernel(name, body, results, inputs, scratch=()):
        products = 2 * groups * query_group * rows * rows * HEAD_SIZE
        return pl.pallas_call(
            functools.partial(body, query_group),
            out_shape=results,
            in_specs=[vmem if x.ndim == 2 else smem for x in inputs],
            out_specs=tuple(vmem for _ in results),
            scratch_shapes=scratch,
            compiler_params=pltpu.CompilerParams(vmem_limit_bytes=16 << 20),
            cost_estimate=pl.CostEstimate(
                flops=4 * products,
                bytes_accessed=sum(x.size * x.dtype.itemsize for x in (*inputs, *results)),
                transcendentals=groups * query_group * rows * rows,
            ),
            name=name,
        )(*inputs)

    wide = (groups * rows, query_group * rows)
    narrow = (groups * 8, query_group * rows)
    stack = shaped((groups * query_group * rows, HEAD_SIZE), jnp.bfloat16)
    joined, plan = pl.pallas_call(
        prepare_kernel,
        out_shape=(shaped((rows, 2 * width), jnp.bfloat16), shaped((count + 2,), jnp.int32)),
        in_specs=[smem, smem, smem, vmem, vmem],
        out_specs=(vmem, smem),
        name="prepare",
    )(span_order, pattern.T, jnp.asarray(route_tables()), keys, values)

    def along(route):
        rounds = [list(enumerate(PERMUTATIONS[name])) for name in route]

        def branch(plan, queries, d_out, joined):
            parts = [lax.ppermute(joined, "ctx", pairs) for pairs in rounds]
            query_stack, grad_stack, weights, d_probs, stats = kernel(
                "own_block",
                own_kernel,
                (
                    stack,
                    stack,
                    shaped(wide, jnp.float32),
                    shaped(wide, jnp.float32),
                    shaped(narrow, jnp.float32),
                ),
                (plan, queries, d_out, joined),
            )
            sent, d_scores, joint = kernel(
                "other_block",
                other_kernel,
                (
                    shaped((rows, 2 * width), jnp.bfloat16),
                    shaped(wide, jnp.bfloat16),
                    shaped(narrow, jnp.float32),
                ),
                (query_stack, grad_stack, stats, *parts),
            )
            returned = [
                lax.ppermute(sent, "ctx", [(target, source) for source, target in pairs])
                for pairs in rounds
            ]
            d_queries, own_grads = kernel(
                "rest",
                rest_kernel,
                (shaped(queries.shape, jnp.bfloat16), shaped((rows, 2 * width), jnp.float32)),
                (
                    query_stack,
                    grad_stack,
                    stats,
                    joined,
                    weights,
                    d_probs,
                    d_scores,
                    joint,
                    *parts,
                ),
                (pltpu.VMEM((rows, width), jnp.bfloat16),),
            )
            for r, terms in enumerate(returned):
                terms = terms.astype(jnp.float32)
                if len(returned) > 1:
                    terms = jnp.where(plan[3 + r] > 0, terms, 0.0)
                own_grads = own_grads + terms
            return (
                d_queries,
                own_grads[:, :width].astype(jnp.bfloat16),
                own_grads[:, width:].astype(jnp.bfloat16),
            )

        return branch

    return lax.switch(plan[0], [along(route) for route in ROUTES], plan, queries, d_out, joined)


def heads_first(dense_matrix, key_value_count):
    return dense_matrix.reshape(
        dense_matrix.shape[0], key_value_count, QUERY_HEADS // KEY_VALUE_HEADS, HEAD_SIZE
    ).transpose(1, 2, 0, 3)


def key_mask(start, count, local_pattern, query_pos, span_order):
    key_blocks = start // BLOCK + jnp.arange(count // BLOCK, dtype=jnp.int32)
    named = jnp.any(local_pattern[:, :, None] == key_blocks[None, None, :], axis=1)
    local_blocks = local_pattern.shape[0]
    named_rows = jnp.broadcast_to(
        named[:, None, :, None], (local_blocks, BLOCK, count // BLOCK, BLOCK)
    )
    named_rows = named_rows.reshape(local_blocks * BLOCK, count)
    key_order = lax.dynamic_slice_in_dim(span_order, start // BLOCK, count // BLOCK, 0)
    key_pos = (key_order[:, None] * BLOCK + jnp.arange(BLOCK, dtype=jnp.int32)[None, :]).reshape(
        count
    )
    return named_rows & (key_pos[None, :] <= query_pos[:, None])


def sweep(step, carry, key_piece, value_piece, start):
    count = key_piece.shape[0]
    width = BLOCK * math.gcd(count // BLOCK, max(1, 512 // BLOCK))
    turns = count // width
    if turns == 1:
        return step(carry, key_piece, value_piece, start)

    def advance(index, inner):
        offset = index * width
        key_part = lax.dynamic_slice_in_dim(key_piece, offset, width, 0)
        value_part = lax.dynamic_slice_in_dim(value_piece, offset, width, 0)
        return step(inner, key_part, value_part, start + offset)

    return lax.fori_loop(0, turns, advance, carry)


def swept(queries, keys, values, d_out, span_order, pattern):
    rows = queries.shape[0]
    key_value_count = keys.shape[1] // HEAD_SIZE
    query_group = QUERY_HEADS // KEY_VALUE_HEADS
    blocks_here = rows // BLOCK
    scale = 1.0 / math.sqrt(HEAD_SIZE)
    first_block = lax.axis_index("ctx") * blocks_here
    local_pattern = lax.dynamic_slice_in_dim(pattern, first_block, blocks_here, 0)
    local_order = lax.dynamic_slice_in_dim(span_order, first_block, blocks_here, 0)
    query_pos = (
        local_order[:, None] * BLOCK + jnp.arange(BLOCK, dtype=jnp.int32)[None, :]
    ).reshape(rows)
    query_heads = heads_first(queries, key_value_count)
    grad_heads = heads_first(d_out, key_value_count)
    total_rows = rows * lax.axis_size("ctx")

    def scores_for(key_piece):
        key_heads = key_piece.reshape(key_piece.shape[0], key_value_count, HEAD_SIZE)
        return (
            jnp.einsum("kgtd,rkd->kgtr", query_heads, key_heads, preferred_element_type=jnp.float32)
            * scale
        )

    def forward_step(carry, key_piece, value_piece, start):
        allowed = key_mask(start, key_piece.shape[0], local_pattern, query_pos, span_order)

        def forward_update(state):
            running_max, total, weighted = state
            scores = scores_for(key_piece)
            new_max = jnp.maximum(running_max, jnp.max(jnp.where(allowed, scores, NEG), axis=-1))
            factor = jnp.exp(running_max - new_max)
            weights = jnp.where(allowed, jnp.exp(scores - new_max[..., None]), 0.0)
            value_heads = value_piece.reshape(
                value_piece.shape[0], key_value_count, HEAD_SIZE
            ).astype(jnp.float32)
            product = jnp.einsum(
                "kgtr,rkd->kgtd", weights, value_heads, precision=lax.Precision.HIGHEST
            )
            return (
                new_max,
                total * factor + jnp.sum(weights, axis=-1),
                weighted * factor[..., None] + product,
            )

        return lax.cond(jnp.any(allowed), forward_update, lambda state: state, carry)

    def make_backward(log_total, delta, anchor):

        def step(carry, key_piece, value_piece, start):
            count = key_piece.shape[0]
            allowed = key_mask(start, count, local_pattern, query_pos, span_order)

            def step_update(state):
                query_grad, key_grads = state
                key_heads = key_piece.reshape(count, key_value_count, HEAD_SIZE)
                value_heads = value_piece.reshape(count, key_value_count, HEAD_SIZE)
                scores = scores_for(key_piece)
                probs = jnp.where(allowed, jnp.exp(scores - log_total[..., None]), 0.0)
                grad_probs = jnp.einsum(
                    "kgtd,rkd->kgtr", grad_heads, value_heads, preferred_element_type=jnp.float32
                )
                grad_scores = (probs * (grad_probs - delta[..., None])).astype(jnp.bfloat16)
                query_grad = query_grad + jnp.einsum(
                    "kgtr,rkd->kgtd", grad_scores, key_heads, preferred_element_type=jnp.float32
                )
                key_part = (
                    jnp.einsum(
                        "kgtr,kgtd->rkd",
                        grad_scores,
                        query_heads,
                        preferred_element_type=jnp.float32,
                    )
                    * scale
                )
                value_part = jnp.einsum(
                    "kgtr,kgtd->rkd",
                    probs.astype(jnp.bfloat16),
                    grad_heads,
                    preferred_element_type=jnp.float32,
                )
                joined = jnp.stack(
                    (
                        key_part.reshape(count, key_value_count * HEAD_SIZE),
                        value_part.reshape(count, key_value_count * HEAD_SIZE),
                    ),
                    axis=1,
                )
                offset = start - anchor
                former = lax.dynamic_slice_in_dim(key_grads, offset, count, 0)
                key_grads = lax.dynamic_update_slice_in_dim(key_grads, former + joined, offset, 0)
                return (query_grad, key_grads)

            return lax.cond(jnp.any(allowed), step_update, lambda state: state, carry)

        return step

    start_state = (
        jnp.full((key_value_count, query_group, rows), NEG, jnp.float32),
        jnp.zeros((key_value_count, query_group, rows), jnp.float32),
        jnp.zeros((key_value_count, query_group, rows, HEAD_SIZE), jnp.float32),
    )
    query_zero = jnp.zeros((key_value_count, query_group, rows, HEAD_SIZE), jnp.float32)
    state = sweep(
        forward_step,
        start_state,
        lax.all_gather(keys, "ctx", axis=0, tiled=True),
        lax.all_gather(values, "ctx", axis=0, tiled=True),
        jnp.int32(0),
    )
    running_max, total, weighted = state
    attended = weighted / total[..., None]
    log_total = running_max + jnp.log(total)
    delta = jnp.sum(grad_heads * attended, axis=-1)
    log_total, delta = (log_total, delta)
    both_step = make_backward(log_total, delta, 0)
    grad_zero = jnp.zeros((total_rows, 2, key_value_count * HEAD_SIZE), jnp.float32)
    query_grad, key_grads = sweep(
        both_step,
        (query_zero, grad_zero),
        lax.all_gather(keys, "ctx", axis=0, tiled=True),
        lax.all_gather(values, "ctx", axis=0, tiled=True),
        jnp.int32(0),
    )
    summed = lax.psum_scatter(key_grads, "ctx", scatter_dimension=0, tiled=True)
    d_queries = (
        (query_grad * scale)
        .transpose(2, 0, 1, 3)
        .reshape(rows, key_value_count * query_group * HEAD_SIZE)
        .astype(jnp.bfloat16)
    )
    key_gradients = summed[:, 0, :].astype(jnp.bfloat16)
    value_gradients = summed[:, 1, :].astype(jnp.bfloat16)
    return (d_queries, key_gradients, value_gradients)


def on_device(queries, keys, values, d_out, span_order, pattern):
    count = lax.axis_size("ctx")
    if count == 4 and keys.shape[0] == BLOCK and pattern.shape == (count, 2):
        return routed(queries, keys, values, d_out, span_order, pattern)
    return swept(queries, keys, values, d_out, span_order, pattern)


def solution(mesh):
    return jax.shard_map(
        on_device,
        mesh=mesh,
        in_specs=(
            P(("grp", "ctx"), "head"),
            P(("grp", "ctx"), "head"),
            P(("grp", "ctx"), "head"),
            P(("grp", "ctx"), "head"),
            P(),
            P(),
        ),
        out_specs=(P(("grp", "ctx"), "head"), P(("grp", "ctx"), "head"), P(("grp", "ctx"), "head")),
        check_vma=False,
    )
```

```python
import functools
import itertools
import math

import jax
import jax.numpy as jnp
import numpy as np
from jax import lax
from jax.experimental import pallas as pl
from jax.experimental.pallas import tpu as pltpu
from jax.sharding import PartitionSpec as P

QUERY_HEADS = 64
KEY_VALUE_HEADS = 8
HEAD_SIZE = 128
BLOCK = 128


NEG = -1e30


PERMUTATIONS = {
    "a": (1, 2, 3, 0),
    "b": (1, 3, 0, 2),
    "c": (2, 0, 3, 1),
    "d": (3, 0, 1, 2),
    "e": (2, 3, 1, 0),
    "f": (3, 2, 0, 1),
    "s": (1, 0, 3, 2),
    "t": (2, 3, 0, 1),
    "u": (3, 2, 1, 0),
}
ROUTES = ("s", "b", "c", "a", "d", "e", "ab", "f", "ac", "bc", "bd", "ad", "dc", "bcu")


def route_tables():
    count = 4
    table = np.zeros(count**count, np.int32)
    sources = np.full((len(ROUTES), count - 1, count), -1, np.int32)
    targets = np.full((len(ROUTES), count - 1, count), -1, np.int32)
    pairs = []
    for k, route in enumerate(ROUTES):
        pairs.append(set())
        for r, name in enumerate(route):
            for source, target in enumerate(PERMUTATIONS[name]):
                if (source, target) not in pairs[k]:
                    sources[k, r, target], targets[k, r, source] = source, target
                    pairs[k].add((source, target))
    for shifts in itertools.product(range(count), repeat=count):
        need = {((i + shift) % count, i) for i, shift in enumerate(shifts) if shift}
        last = {i for i in range(count) if not shifts[i]}
        for _ in range(count):
            last |= {target for source, target in need if source in last}
        if len(last) == count:
            code = sum(shift * count**i for i, shift in enumerate(shifts))
            table[code] = next(k for k, held in enumerate(pairs) if need <= held)
    return np.concatenate((table, sources.ravel(), targets.ravel()))


def prepare_kernel(order_ref, pattern_ref, table_ref, keys_ref, values_ref, joined_ref, plan_ref):
    count = pattern_ref.shape[1]
    code = jnp.int32(0)
    for i in range(count):
        other = pattern_ref[1, i]
        shift = jnp.where(other < i, other - i + count, other - i)
        code += jnp.where(order_ref[other] < order_ref[i], shift, 0) * count**i
    route = table_ref[code]
    block = lax.axis_index("ctx")
    mine = pattern_ref[1, block]
    plan_ref[0] = route
    take = jnp.int32(0)
    for r in range(count - 1):
        place = count**count + (route * (count - 1) + r) * count + block
        take = jnp.where(table_ref[place] == mine, r, take)
        reader = table_ref[place + len(ROUTES) * (count - 1) * count]
        at = jnp.maximum(reader, 0)
        wanted = (reader >= 0) & (pattern_ref[1, at] == block)
        plan_ref[3 + r] = wanted.astype(jnp.int32)
    plan_ref[1] = take
    plan_ref[2] = (order_ref[mine] < order_ref[block]).astype(jnp.int32)
    width = keys_ref.shape[1]
    joined_ref[:, :width] = keys_ref[...]
    joined_ref[:, width:] = values_ref[...]


def span(start, size):
    if isinstance(start, int):
        return slice(start, start + size)
    return pl.ds(pl.multiple_of(start, size), size)


def columns_of(group, width, query_group):
    start = group * HEAD_SIZE
    heads = [span((group * query_group + head) * HEAD_SIZE, HEAD_SIZE) for head in range(query_group)]
    return span(start, HEAD_SIZE), span(width + start, HEAD_SIZE), heads


def stacked(ref, heads):
    return jnp.concatenate([ref[:, head] for head in heads], axis=0)


def against(rows, columns):
    return lax.dot_general(
        rows, columns, (((1,), (1,)), ((), ())), preferred_element_type=jnp.float32
    )


def picked(turn, choices):
    chosen = choices[0]
    for r in range(1, len(choices)):
        chosen = jnp.where(jnp.broadcast_to(turn[:, : chosen.shape[1]], chosen.shape) == r, choices[r], chosen)
    return chosen


LOG2_SCALE = math.log2(math.e) / math.sqrt(HEAD_SIZE)
SCALE = 1.0 / math.sqrt(HEAD_SIZE)


def own_kernel(
    query_group,
    plan_ref,
    queries_ref,
    grads_ref,
    own_ref,
    query_stack_ref,
    grad_stack_ref,
    weights_ref,
    d_probs_ref,
    stats_ref,
):
    rule = jnp.where(plan_ref[2] > 0, 0.0, jnp.full((1, stats_ref.shape[1]), NEG))
    turn = jnp.full((1, stats_ref.shape[1]), plan_ref[1].astype(jnp.float32))
    adds = [jnp.full((1, stats_ref.shape[1]), plan_ref[3 + r].astype(jnp.float32)) for r in range(3)]
    rows = queries_ref.shape[0]
    width = own_ref.shape[1] // 2
    shape = (rows, query_group * rows)
    allowed = lax.broadcasted_iota(jnp.int32, shape, 0) <= (
        lax.broadcasted_iota(jnp.int32, shape, 1) % rows
    )
    bias = jnp.where(allowed, 0.0, NEG)

    @pl.loop(0, width // HEAD_SIZE)
    def _(group):
        key_columns, value_columns, heads = columns_of(group, width, query_group)
        block = span(group * rows, rows)
        stack = span(group * query_group * rows, query_group * rows)
        query, grad = stacked(queries_ref, heads), stacked(grads_ref, heads)
        query_stack_ref[stack], grad_stack_ref[stack] = query, grad
        scores = against(own_ref[:, key_columns], query) * LOG2_SCALE + bias
        top = jnp.max(scores, axis=0, keepdims=True)
        weights = jnp.exp2(scores - top)
        d_probs = against(own_ref[:, value_columns], grad)
        weights_ref[block] = weights
        d_probs_ref[block] = d_probs
        total = jnp.sum(weights, axis=0, keepdims=True)
        delta = jnp.sum(weights * d_probs, axis=0, keepdims=True)
        stats_ref[span(group * 8, 8)] = jnp.concatenate((top, total, delta, rule, turn, *adds))


def other_kernel(
    query_group,
    unrolled,
    queries_ref,
    grads_ref,
    stats_ref,
    other_ref,
    sent_ref,
    d_scores_ref,
    joint_ref,
):
    rows, width = other_ref.shape[0], other_ref.shape[1] // 2
    groups = width // HEAD_SIZE

    def products(group):
        key_columns, value_columns, _ = columns_of(group, width, query_group)
        stack = span(group * query_group * rows, query_group * rows)
        return (
            against(other_ref[:, key_columns], queries_ref[stack]),
            against(other_ref[:, value_columns], grads_ref[stack]),
        )

    def step(group, scores, d_probs):
        key_columns, value_columns, _ = columns_of(group, width, query_group)
        stack = span(group * query_group * rows, query_group * rows)
        stats = stats_ref[span(group * 8, 8)]
        own_top, own_total, own_delta, bias = (stats[k : k + 1] for k in range(4))
        scores = scores * LOG2_SCALE + bias
        top = jnp.maximum(own_top, jnp.max(scores, axis=0, keepdims=True))
        factor = jnp.exp2(own_top - top)
        weights = jnp.exp2(scores - top)
        inverse = 1.0 / (own_total * factor + jnp.sum(weights, axis=0, keepdims=True))
        delta = (own_delta * factor + jnp.sum(weights * d_probs, axis=0, keepdims=True)) * inverse
        probs = weights * inverse
        d_scores = (probs * (d_probs - delta)).astype(jnp.bfloat16)
        d_scores_ref[span(group * rows, rows)] = d_scores
        blank = jnp.zeros((6, delta.shape[1]), jnp.float32)
        joint_ref[span(group * 8, 8)] = jnp.concatenate((factor * inverse, delta, blank))
        d_key = jnp.dot(d_scores, queries_ref[stack], preferred_element_type=jnp.float32) * SCALE
        d_value = jnp.dot(
            probs.astype(jnp.bfloat16), grads_ref[stack], preferred_element_type=jnp.float32
        )
        sent_ref[:, key_columns] = d_key.astype(jnp.bfloat16)
        sent_ref[:, value_columns] = d_value.astype(jnp.bfloat16)

    if unrolled:
        for group, made in enumerate([products(group) for group in range(groups)]):
            step(group, *made)
    else:
        pl.loop(0, groups)(lambda group: step(group, *products(group)))


def rest_kernel(
    query_group,
    rounds,
    queries_ref,
    grads_ref,
    stats_ref,
    own_ref,
    weights_ref,
    d_probs_ref,
    *refs,
):
    part_refs, d_scores_refs, joint_refs = (refs[k * rounds : (k + 1) * rounds] for k in range(3))
    d_queries_ref, own_grads_ref = refs[3 * rounds :]
    rows, width = own_ref.shape[0], own_ref.shape[1] // 2

    @pl.loop(0, width // HEAD_SIZE)
    def _(group):
        key_columns, value_columns, heads = columns_of(group, width, query_group)
        block = span(group * rows, rows)
        stack = span(group * query_group * rows, query_group * rows)
        query, grad = queries_ref[stack], grads_ref[stack]
        turn = stats_ref[span(group * 8, 8)][4:5]
        joint = picked(turn, [ref[span(group * 8, 8)] for ref in joint_refs])
        probs = weights_ref[block] * joint[:1]
        d_scores = (probs * (d_probs_ref[block] - joint[1:2])).astype(jnp.bfloat16)
        d_key = jnp.dot(d_scores, query, preferred_element_type=jnp.float32) * SCALE
        d_value = jnp.dot(probs.astype(jnp.bfloat16), grad, preferred_element_type=jnp.float32)
        own_grads_ref[:, key_columns] = d_key
        own_grads_ref[:, value_columns] = d_value
        other_key = picked(turn, [ref[:, key_columns] for ref in part_refs])
        both = jnp.concatenate((d_scores, picked(turn, [ref[block] for ref in d_scores_refs])), axis=0)
        key = jnp.concatenate((own_ref[:, key_columns], other_key), axis=0)
        d_query = lax.dot_general(
            both, key, (((0,), (0,)), ((), ())), preferred_element_type=jnp.float32
        )
        d_query = (d_query * SCALE).astype(jnp.bfloat16)
        for index, head in enumerate(heads):
            d_queries_ref[:, head] = d_query[index * rows : (index + 1) * rows]


def routed(queries, keys, values, d_out, span_order, pattern):
    rows, width = keys.shape
    count = pattern.shape[0]
    query_group = QUERY_HEADS // KEY_VALUE_HEADS
    groups = width // HEAD_SIZE
    smem = pl.BlockSpec(memory_space=pltpu.SMEM)
    vmem = pl.BlockSpec(memory_space=pltpu.VMEM)

    def shaped(shape, dtype):
        return jax.ShapeDtypeStruct(shape, dtype)

    def kernel(name, body, results, inputs):
        products = 2 * groups * query_group * rows * rows * HEAD_SIZE
        return pl.pallas_call(
            functools.partial(body, query_group),
            out_shape=results,
            in_specs=[vmem if x.ndim == 2 else smem for x in inputs],
            out_specs=tuple(vmem for _ in results),
            compiler_params=pltpu.CompilerParams(vmem_limit_bytes=16 << 20),
            cost_estimate=pl.CostEstimate(
                flops=4 * products,
                bytes_accessed=sum(x.size * x.dtype.itemsize for x in (*inputs, *results)),
                transcendentals=groups * query_group * rows * rows,
            ),
            name=name,
        )(*inputs)

    wide = (groups * rows, query_group * rows)
    narrow = (groups * 8, query_group * rows)
    stack = shaped((groups * query_group * rows, HEAD_SIZE), jnp.bfloat16)
    joined, plan = pl.pallas_call(
        prepare_kernel,
        out_shape=(shaped((rows, 2 * width), jnp.bfloat16), shaped((count + 2,), jnp.int32)),
        in_specs=[smem, smem, smem, vmem, vmem],
        out_specs=(vmem, smem),
        name="prepare",
    )(span_order, pattern.T, jnp.asarray(route_tables()), keys, values)

    def along(route):
        rounds = [list(enumerate(PERMUTATIONS[name])) for name in route]

        def branch(plan, queries, d_out, joined):
            parts = [lax.ppermute(joined, "ctx", pairs) for pairs in rounds]
            query_stack, grad_stack, weights, d_probs, stats = kernel(
                "own_block",
                own_kernel,
                (
                    stack,
                    stack,
                    shaped(wide, jnp.float32),
                    shaped(wide, jnp.float32),
                    shaped(narrow, jnp.float32),
                ),
                (plan, queries, d_out, joined),
            )
            returned, d_scores, joints = [], [], []
            for part, pairs in zip(parts, rounds):
                sent, d_score, joint = kernel(
                    "other_block",
                    lambda query_group, *refs: other_kernel(query_group, len(rounds) == 1, *refs),
                    (
                        shaped((rows, 2 * width), jnp.bfloat16),
                        shaped(wide, jnp.bfloat16),
                        shaped(narrow, jnp.float32),
                    ),
                    (query_stack, grad_stack, stats, part),
                )
                back = [(target, source) for source, target in pairs]
                returned.append(lax.ppermute(sent, "ctx", back))
                d_scores.append(d_score)
                joints.append(joint)
            own = (query_stack, grad_stack, stats, joined, weights, d_probs)
            d_queries, own_grads = kernel(
                "rest",
                lambda query_group, *refs: rest_kernel(query_group, len(rounds), *refs),
                (shaped(queries.shape, jnp.bfloat16), shaped((rows, 2 * width), jnp.float32)),
                (*own, *parts, *d_scores, *joints),
            )
            for r, terms in enumerate(returned):
                terms = terms.astype(jnp.float32)
                if len(returned) > 1:
                    terms = jnp.where(stats[5 + r : 6 + r, : 2 * width] > 0.0, terms, 0.0)
                own_grads = own_grads + terms
            return (
                d_queries,
                own_grads[:, :width].astype(jnp.bfloat16),
                own_grads[:, width:].astype(jnp.bfloat16),
            )

        return branch

    return lax.switch(plan[0], [along(route) for route in ROUTES], plan, queries, d_out, joined)


def heads_first(dense_matrix, key_value_count):
    return dense_matrix.reshape(
        dense_matrix.shape[0], key_value_count, QUERY_HEADS // KEY_VALUE_HEADS, HEAD_SIZE
    ).transpose(1, 2, 0, 3)


def key_mask(start, count, local_pattern, query_pos, span_order):
    key_blocks = start // BLOCK + jnp.arange(count // BLOCK, dtype=jnp.int32)
    named = jnp.any(local_pattern[:, :, None] == key_blocks[None, None, :], axis=1)
    local_blocks = local_pattern.shape[0]
    named_rows = jnp.broadcast_to(
        named[:, None, :, None], (local_blocks, BLOCK, count // BLOCK, BLOCK)
    )
    named_rows = named_rows.reshape(local_blocks * BLOCK, count)
    key_order = lax.dynamic_slice_in_dim(span_order, start // BLOCK, count // BLOCK, 0)
    key_pos = (key_order[:, None] * BLOCK + jnp.arange(BLOCK, dtype=jnp.int32)[None, :]).reshape(
        count
    )
    return named_rows & (key_pos[None, :] <= query_pos[:, None])


def sweep(step, carry, key_piece, value_piece, start):
    count = key_piece.shape[0]
    width = BLOCK * math.gcd(count // BLOCK, max(1, 512 // BLOCK))
    turns = count // width
    if turns == 1:
        return step(carry, key_piece, value_piece, start)

    def advance(index, inner):
        offset = index * width
        key_part = lax.dynamic_slice_in_dim(key_piece, offset, width, 0)
        value_part = lax.dynamic_slice_in_dim(value_piece, offset, width, 0)
        return step(inner, key_part, value_part, start + offset)

    return lax.fori_loop(0, turns, advance, carry)


def swept(queries, keys, values, d_out, span_order, pattern):
    rows = queries.shape[0]
    key_value_count = keys.shape[1] // HEAD_SIZE
    query_group = QUERY_HEADS // KEY_VALUE_HEADS
    blocks_here = rows // BLOCK
    scale = 1.0 / math.sqrt(HEAD_SIZE)
    first_block = lax.axis_index("ctx") * blocks_here
    local_pattern = lax.dynamic_slice_in_dim(pattern, first_block, blocks_here, 0)
    local_order = lax.dynamic_slice_in_dim(span_order, first_block, blocks_here, 0)
    query_pos = (
        local_order[:, None] * BLOCK + jnp.arange(BLOCK, dtype=jnp.int32)[None, :]
    ).reshape(rows)
    query_heads = heads_first(queries, key_value_count)
    grad_heads = heads_first(d_out, key_value_count)
    total_rows = rows * lax.axis_size("ctx")

    def scores_for(key_piece):
        key_heads = key_piece.reshape(key_piece.shape[0], key_value_count, HEAD_SIZE)
        return (
            jnp.einsum("kgtd,rkd->kgtr", query_heads, key_heads, preferred_element_type=jnp.float32)
            * scale
        )

    def forward_step(carry, key_piece, value_piece, start):
        allowed = key_mask(start, key_piece.shape[0], local_pattern, query_pos, span_order)

        def forward_update(state):
            running_max, total, weighted = state
            scores = scores_for(key_piece)
            new_max = jnp.maximum(running_max, jnp.max(jnp.where(allowed, scores, NEG), axis=-1))
            factor = jnp.exp(running_max - new_max)
            weights = jnp.where(allowed, jnp.exp(scores - new_max[..., None]), 0.0)
            value_heads = value_piece.reshape(
                value_piece.shape[0], key_value_count, HEAD_SIZE
            ).astype(jnp.float32)
            product = jnp.einsum(
                "kgtr,rkd->kgtd", weights, value_heads, precision=lax.Precision.HIGHEST
            )
            return (
                new_max,
                total * factor + jnp.sum(weights, axis=-1),
                weighted * factor[..., None] + product,
            )

        return lax.cond(jnp.any(allowed), forward_update, lambda state: state, carry)

    def make_backward(log_total, delta, anchor):

        def step(carry, key_piece, value_piece, start):
            count = key_piece.shape[0]
            allowed = key_mask(start, count, local_pattern, query_pos, span_order)

            def step_update(state):
                query_grad, key_grads = state
                key_heads = key_piece.reshape(count, key_value_count, HEAD_SIZE)
                value_heads = value_piece.reshape(count, key_value_count, HEAD_SIZE)
                scores = scores_for(key_piece)
                probs = jnp.where(allowed, jnp.exp(scores - log_total[..., None]), 0.0)
                grad_probs = jnp.einsum(
                    "kgtd,rkd->kgtr", grad_heads, value_heads, preferred_element_type=jnp.float32
                )
                grad_scores = (probs * (grad_probs - delta[..., None])).astype(jnp.bfloat16)
                query_grad = query_grad + jnp.einsum(
                    "kgtr,rkd->kgtd", grad_scores, key_heads, preferred_element_type=jnp.float32
                )
                key_part = (
                    jnp.einsum(
                        "kgtr,kgtd->rkd",
                        grad_scores,
                        query_heads,
                        preferred_element_type=jnp.float32,
                    )
                    * scale
                )
                value_part = jnp.einsum(
                    "kgtr,kgtd->rkd",
                    probs.astype(jnp.bfloat16),
                    grad_heads,
                    preferred_element_type=jnp.float32,
                )
                joined = jnp.stack(
                    (
                        key_part.reshape(count, key_value_count * HEAD_SIZE),
                        value_part.reshape(count, key_value_count * HEAD_SIZE),
                    ),
                    axis=1,
                )
                offset = start - anchor
                former = lax.dynamic_slice_in_dim(key_grads, offset, count, 0)
                key_grads = lax.dynamic_update_slice_in_dim(key_grads, former + joined, offset, 0)
                return (query_grad, key_grads)

            return lax.cond(jnp.any(allowed), step_update, lambda state: state, carry)

        return step

    start_state = (
        jnp.full((key_value_count, query_group, rows), NEG, jnp.float32),
        jnp.zeros((key_value_count, query_group, rows), jnp.float32),
        jnp.zeros((key_value_count, query_group, rows, HEAD_SIZE), jnp.float32),
    )
    query_zero = jnp.zeros((key_value_count, query_group, rows, HEAD_SIZE), jnp.float32)
    state = sweep(
        forward_step,
        start_state,
        lax.all_gather(keys, "ctx", axis=0, tiled=True),
        lax.all_gather(values, "ctx", axis=0, tiled=True),
        jnp.int32(0),
    )
    running_max, total, weighted = state
    attended = weighted / total[..., None]
    log_total = running_max + jnp.log(total)
    delta = jnp.sum(grad_heads * attended, axis=-1)
    log_total, delta = (log_total, delta)
    both_step = make_backward(log_total, delta, 0)
    grad_zero = jnp.zeros((total_rows, 2, key_value_count * HEAD_SIZE), jnp.float32)
    query_grad, key_grads = sweep(
        both_step,
        (query_zero, grad_zero),
        lax.all_gather(keys, "ctx", axis=0, tiled=True),
        lax.all_gather(values, "ctx", axis=0, tiled=True),
        jnp.int32(0),
    )
    summed = lax.psum_scatter(key_grads, "ctx", scatter_dimension=0, tiled=True)
    d_queries = (
        (query_grad * scale)
        .transpose(2, 0, 1, 3)
        .reshape(rows, key_value_count * query_group * HEAD_SIZE)
        .astype(jnp.bfloat16)
    )
    key_gradients = summed[:, 0, :].astype(jnp.bfloat16)
    value_gradients = summed[:, 1, :].astype(jnp.bfloat16)
    return (d_queries, key_gradients, value_gradients)


def on_device(queries, keys, values, d_out, span_order, pattern):
    count = lax.axis_size("ctx")
    if count == 4 and keys.shape[0] == BLOCK and pattern.shape == (count, 2):
        return routed(queries, keys, values, d_out, span_order, pattern)
    return swept(queries, keys, values, d_out, span_order, pattern)


def solution(mesh):
    return jax.shard_map(
        on_device,
        mesh=mesh,
        in_specs=(
            P(("grp", "ctx"), "head"),
            P(("grp", "ctx"), "head"),
            P(("grp", "ctx"), "head"),
            P(("grp", "ctx"), "head"),
            P(),
            P(),
        ),
        out_specs=(P(("grp", "ctx"), "head"), P(("grp", "ctx"), "head"), P(("grp", "ctx"), "head")),
        check_vma=False,
    )
```

```python
import functools
import itertools
import math

import jax
import jax.numpy as jnp
import numpy as np
from jax import lax
from jax.experimental import pallas as pl
from jax.experimental.pallas import tpu as pltpu
from jax.sharding import PartitionSpec as P

QUERY_HEADS = 64
KEY_VALUE_HEADS = 8
HEAD_SIZE = 128
BLOCK = 128


NEG = -1e30


PERMUTATIONS = {
    "a": (1, 2, 3, 0),
    "b": (1, 3, 0, 2),
    "c": (2, 0, 3, 1),
    "d": (3, 0, 1, 2),
    "e": (2, 3, 1, 0),
    "f": (3, 2, 0, 1),
    "s": (1, 0, 3, 2),
    "t": (2, 3, 0, 1),
    "u": (3, 2, 1, 0),
}
ROUTES = ("s", "b", "c", "a", "d", "e", "ab", "f", "ac", "bc", "bd", "ad", "dc", "ubc")


def route_tables():
    count = 4
    table = np.zeros(count**count, np.int32)
    sources = np.full((len(ROUTES), count - 1, count), -1, np.int32)
    targets = np.full((len(ROUTES), count - 1, count), -1, np.int32)
    pairs = []
    for k, route in enumerate(ROUTES):
        pairs.append(set())
        for r, name in enumerate(route):
            for source, target in enumerate(PERMUTATIONS[name]):
                if (source, target) not in pairs[k]:
                    sources[k, r, target], targets[k, r, source] = source, target
                    pairs[k].add((source, target))
    for shifts in itertools.product(range(count), repeat=count):
        need = {((i + shift) % count, i) for i, shift in enumerate(shifts) if shift}
        last = {i for i in range(count) if not shifts[i]}
        for _ in range(count):
            last |= {target for source, target in need if source in last}
        if len(last) == count:
            code = sum(shift * count**i for i, shift in enumerate(shifts))
            table[code] = next(k for k, held in enumerate(pairs) if need <= held)
    return np.concatenate((table, sources.ravel(), targets.ravel()))


def prepare_kernel(order_ref, pattern_ref, table_ref, keys_ref, values_ref, joined_ref, plan_ref):
    count = pattern_ref.shape[1]
    code = jnp.int32(0)
    for i in range(count):
        other = pattern_ref[1, i]
        shift = jnp.where(other < i, other - i + count, other - i)
        code += jnp.where(order_ref[other] < order_ref[i], shift, 0) * count**i
    route = table_ref[code]
    block = lax.axis_index("ctx")
    mine = pattern_ref[1, block]
    plan_ref[0] = route
    take = jnp.int32(0)
    for r in range(count - 1):
        place = count**count + (route * (count - 1) + r) * count + block
        take = jnp.where(table_ref[place] == mine, r, take)
        reader = table_ref[place + len(ROUTES) * (count - 1) * count]
        at = jnp.maximum(reader, 0)
        wanted = (reader >= 0) & (pattern_ref[1, at] == block)
        plan_ref[3 + r] = wanted.astype(jnp.int32)
    plan_ref[1] = take
    plan_ref[2] = (order_ref[mine] < order_ref[block]).astype(jnp.int32)
    width = keys_ref.shape[1]
    joined_ref[:, :width] = keys_ref[...]
    joined_ref[:, width:] = values_ref[...]


def span(start, size):
    if isinstance(start, int):
        return slice(start, start + size)
    return pl.ds(pl.multiple_of(start, size), size)


def columns_of(group, width, query_group):
    start = group * HEAD_SIZE
    heads = [span((group * query_group + head) * HEAD_SIZE, HEAD_SIZE) for head in range(query_group)]
    return span(start, HEAD_SIZE), span(width + start, HEAD_SIZE), heads


def stacked(ref, heads):
    return jnp.concatenate([ref[:, head] for head in heads], axis=0)


def against(rows, columns):
    return lax.dot_general(
        rows, columns, (((1,), (1,)), ((), ())), preferred_element_type=jnp.float32
    )


def picked(turn, choices):
    chosen = choices[0]
    for r in range(1, len(choices)):
        chosen = jnp.where(jnp.broadcast_to(turn[:, : chosen.shape[1]], chosen.shape) == r, choices[r], chosen)
    return chosen


LOG2_SCALE = math.log2(math.e) / math.sqrt(HEAD_SIZE)
SCALE = 1.0 / math.sqrt(HEAD_SIZE)


def own_kernel(
    query_group,
    plan_ref,
    queries_ref,
    grads_ref,
    own_ref,
    query_stack_ref,
    grad_stack_ref,
    weights_ref,
    d_probs_ref,
    stats_ref,
):
    rule = jnp.where(plan_ref[2] > 0, 0.0, jnp.full((1, stats_ref.shape[1]), NEG))
    turn = jnp.full((1, stats_ref.shape[1]), plan_ref[1].astype(jnp.float32))
    adds = [jnp.full((1, stats_ref.shape[1]), plan_ref[3 + r].astype(jnp.float32)) for r in range(3)]
    rows = queries_ref.shape[0]
    width = own_ref.shape[1] // 2
    shape = (rows, query_group * rows)
    allowed = lax.broadcasted_iota(jnp.int32, shape, 0) <= (
        lax.broadcasted_iota(jnp.int32, shape, 1) % rows
    )
    bias = jnp.where(allowed, 0.0, NEG)

    @pl.loop(0, width // HEAD_SIZE)
    def _(group):
        key_columns, value_columns, heads = columns_of(group, width, query_group)
        block = span(group * rows, rows)
        stack = span(group * query_group * rows, query_group * rows)
        query, grad = stacked(queries_ref, heads), stacked(grads_ref, heads)
        query_stack_ref[stack], grad_stack_ref[stack] = query, grad
        scores = against(own_ref[:, key_columns], query) * LOG2_SCALE + bias
        top = jnp.max(scores, axis=0, keepdims=True)
        weights = jnp.exp2(scores - top)
        d_probs = against(own_ref[:, value_columns], grad)
        weights_ref[block] = weights
        d_probs_ref[block] = d_probs
        total = jnp.sum(weights, axis=0, keepdims=True)
        delta = jnp.sum(weights * d_probs, axis=0, keepdims=True)
        stats_ref[span(group * 8, 8)] = jnp.concatenate((top, total, delta, rule, turn, *adds))


def other_kernel(
    query_group,
    unrolled,
    queries_ref,
    grads_ref,
    stats_ref,
    other_ref,
    sent_ref,
    d_scores_ref,
    joint_ref,
):
    rows, width = other_ref.shape[0], other_ref.shape[1] // 2
    groups = width // HEAD_SIZE

    def products(group):
        key_columns, value_columns, _ = columns_of(group, width, query_group)
        stack = span(group * query_group * rows, query_group * rows)
        return (
            against(other_ref[:, key_columns], queries_ref[stack]),
            against(other_ref[:, value_columns], grads_ref[stack]),
        )

    def step(group, scores, d_probs):
        key_columns, value_columns, _ = columns_of(group, width, query_group)
        stack = span(group * query_group * rows, query_group * rows)
        stats = stats_ref[span(group * 8, 8)]
        own_top, own_total, own_delta, bias = (stats[k : k + 1] for k in range(4))
        scores = scores * LOG2_SCALE + bias
        top = jnp.maximum(own_top, jnp.max(scores, axis=0, keepdims=True))
        factor = jnp.exp2(own_top - top)
        weights = jnp.exp2(scores - top)
        inverse = 1.0 / (own_total * factor + jnp.sum(weights, axis=0, keepdims=True))
        delta = (own_delta * factor + jnp.sum(weights * d_probs, axis=0, keepdims=True)) * inverse
        probs = weights * inverse
        d_scores = (probs * (d_probs - delta)).astype(jnp.bfloat16)
        d_scores_ref[span(group * rows, rows)] = d_scores
        blank = jnp.zeros((6, delta.shape[1]), jnp.float32)
        joint_ref[span(group * 8, 8)] = jnp.concatenate((factor * inverse, delta, blank))
        d_key = jnp.dot(d_scores, queries_ref[stack], preferred_element_type=jnp.float32) * SCALE
        d_value = jnp.dot(
            probs.astype(jnp.bfloat16), grads_ref[stack], preferred_element_type=jnp.float32
        )
        sent_ref[:, key_columns] = d_key.astype(jnp.bfloat16)
        sent_ref[:, value_columns] = d_value.astype(jnp.bfloat16)

    if unrolled:
        for group, made in enumerate([products(group) for group in range(groups)]):
            step(group, *made)
    else:
        pl.loop(0, groups)(lambda group: step(group, *products(group)))


def rest_kernel(
    query_group,
    rounds,
    queries_ref,
    grads_ref,
    stats_ref,
    own_ref,
    weights_ref,
    d_probs_ref,
    *refs,
):
    part_refs, d_scores_refs, joint_refs = (refs[k * rounds : (k + 1) * rounds] for k in range(3))
    d_queries_ref, own_grads_ref = refs[3 * rounds :]
    rows, width = own_ref.shape[0], own_ref.shape[1] // 2

    @pl.loop(0, width // HEAD_SIZE)
    def _(group):
        key_columns, value_columns, heads = columns_of(group, width, query_group)
        block = span(group * rows, rows)
        stack = span(group * query_group * rows, query_group * rows)
        query, grad = queries_ref[stack], grads_ref[stack]
        turn = stats_ref[span(group * 8, 8)][4:5]
        joint = picked(turn, [ref[span(group * 8, 8)] for ref in joint_refs])
        probs = weights_ref[block] * joint[:1]
        d_scores = (probs * (d_probs_ref[block] - joint[1:2])).astype(jnp.bfloat16)
        d_key = jnp.dot(d_scores, query, preferred_element_type=jnp.float32) * SCALE
        d_value = jnp.dot(probs.astype(jnp.bfloat16), grad, preferred_element_type=jnp.float32)
        own_grads_ref[:, key_columns] = d_key
        own_grads_ref[:, value_columns] = d_value
        other_key = picked(turn, [ref[:, key_columns] for ref in part_refs])
        both = jnp.concatenate((d_scores, picked(turn, [ref[block] for ref in d_scores_refs])), axis=0)
        key = jnp.concatenate((own_ref[:, key_columns], other_key), axis=0)
        d_query = lax.dot_general(
            both, key, (((0,), (0,)), ((), ())), preferred_element_type=jnp.float32
        )
        d_query = (d_query * SCALE).astype(jnp.bfloat16)
        for index, head in enumerate(heads):
            d_queries_ref[:, head] = d_query[index * rows : (index + 1) * rows]


def routed(queries, keys, values, d_out, span_order, pattern):
    rows, width = keys.shape
    count = pattern.shape[0]
    query_group = QUERY_HEADS // KEY_VALUE_HEADS
    groups = width // HEAD_SIZE
    smem = pl.BlockSpec(memory_space=pltpu.SMEM)
    vmem = pl.BlockSpec(memory_space=pltpu.VMEM)

    def shaped(shape, dtype):
        return jax.ShapeDtypeStruct(shape, dtype)

    def kernel(name, body, results, inputs):
        products = 2 * groups * query_group * rows * rows * HEAD_SIZE
        return pl.pallas_call(
            functools.partial(body, query_group),
            out_shape=results,
            in_specs=[vmem if x.ndim == 2 else smem for x in inputs],
            out_specs=tuple(vmem for _ in results),
            compiler_params=pltpu.CompilerParams(vmem_limit_bytes=16 << 20),
            cost_estimate=pl.CostEstimate(
                flops=4 * products,
                bytes_accessed=sum(x.size * x.dtype.itemsize for x in (*inputs, *results)),
                transcendentals=groups * query_group * rows * rows,
            ),
            name=name,
        )(*inputs)

    wide = (groups * rows, query_group * rows)
    narrow = (groups * 8, query_group * rows)
    stack = shaped((groups * query_group * rows, HEAD_SIZE), jnp.bfloat16)
    joined, plan = pl.pallas_call(
        prepare_kernel,
        out_shape=(shaped((rows, 2 * width), jnp.bfloat16), shaped((count + 2,), jnp.int32)),
        in_specs=[smem, smem, smem, vmem, vmem],
        out_specs=(vmem, smem),
        name="prepare",
    )(span_order, pattern.T, jnp.asarray(route_tables()), keys, values)

    def along(route):
        rounds = [list(enumerate(PERMUTATIONS[name])) for name in route]

        def branch(plan, queries, d_out, joined):
            parts = [lax.ppermute(joined, "ctx", pairs) for pairs in rounds]
            query_stack, grad_stack, weights, d_probs, stats = kernel(
                "own_block",
                own_kernel,
                (
                    stack,
                    stack,
                    shaped(wide, jnp.float32),
                    shaped(wide, jnp.float32),
                    shaped(narrow, jnp.float32),
                ),
                (plan, queries, d_out, joined),
            )
            returned, d_scores, joints = [], [], []
            for part, pairs in zip(parts, rounds):
                sent, d_score, joint = kernel(
                    "other_block",
                    lambda query_group, *refs: other_kernel(query_group, len(rounds) == 1, *refs),
                    (
                        shaped((rows, 2 * width), jnp.bfloat16),
                        shaped(wide, jnp.bfloat16),
                        shaped(narrow, jnp.float32),
                    ),
                    (query_stack, grad_stack, stats, part),
                )
                back = [(target, source) for source, target in pairs]
                returned.append(lax.ppermute(sent, "ctx", back))
                d_scores.append(d_score)
                joints.append(joint)
            own = (query_stack, grad_stack, stats, joined, weights, d_probs)
            d_queries, own_grads = kernel(
                "rest",
                lambda query_group, *refs: rest_kernel(query_group, len(rounds), *refs),
                (shaped(queries.shape, jnp.bfloat16), shaped((rows, 2 * width), jnp.float32)),
                (*own, *parts, *d_scores, *joints),
            )
            for r, terms in enumerate(returned):
                terms = terms.astype(jnp.float32)
                if len(returned) > 1:
                    terms = jnp.where(stats[5 + r : 6 + r, : 2 * width] > 0.0, terms, 0.0)
                own_grads = own_grads + terms
            return (
                d_queries,
                own_grads[:, :width].astype(jnp.bfloat16),
                own_grads[:, width:].astype(jnp.bfloat16),
            )

        return branch

    return lax.switch(plan[0], [along(route) for route in ROUTES], plan, queries, d_out, joined)


def heads_first(dense_matrix, key_value_count):
    return dense_matrix.reshape(
        dense_matrix.shape[0], key_value_count, QUERY_HEADS // KEY_VALUE_HEADS, HEAD_SIZE
    ).transpose(1, 2, 0, 3)


def key_mask(start, count, local_pattern, query_pos, span_order):
    key_blocks = start // BLOCK + jnp.arange(count // BLOCK, dtype=jnp.int32)
    named = jnp.any(local_pattern[:, :, None] == key_blocks[None, None, :], axis=1)
    local_blocks = local_pattern.shape[0]
    named_rows = jnp.broadcast_to(
        named[:, None, :, None], (local_blocks, BLOCK, count // BLOCK, BLOCK)
    )
    named_rows = named_rows.reshape(local_blocks * BLOCK, count)
    key_order = lax.dynamic_slice_in_dim(span_order, start // BLOCK, count // BLOCK, 0)
    key_pos = (key_order[:, None] * BLOCK + jnp.arange(BLOCK, dtype=jnp.int32)[None, :]).reshape(
        count
    )
    return named_rows & (key_pos[None, :] <= query_pos[:, None])


def sweep(step, carry, key_piece, value_piece, start):
    count = key_piece.shape[0]
    width = BLOCK * math.gcd(count // BLOCK, max(1, 512 // BLOCK))
    turns = count // width
    if turns == 1:
        return step(carry, key_piece, value_piece, start)

    def advance(index, inner):
        offset = index * width
        key_part = lax.dynamic_slice_in_dim(key_piece, offset, width, 0)
        value_part = lax.dynamic_slice_in_dim(value_piece, offset, width, 0)
        return step(inner, key_part, value_part, start + offset)

    return lax.fori_loop(0, turns, advance, carry)


def swept(queries, keys, values, d_out, span_order, pattern):
    rows = queries.shape[0]
    key_value_count = keys.shape[1] // HEAD_SIZE
    query_group = QUERY_HEADS // KEY_VALUE_HEADS
    blocks_here = rows // BLOCK
    scale = 1.0 / math.sqrt(HEAD_SIZE)
    first_block = lax.axis_index("ctx") * blocks_here
    local_pattern = lax.dynamic_slice_in_dim(pattern, first_block, blocks_here, 0)
    local_order = lax.dynamic_slice_in_dim(span_order, first_block, blocks_here, 0)
    query_pos = (
        local_order[:, None] * BLOCK + jnp.arange(BLOCK, dtype=jnp.int32)[None, :]
    ).reshape(rows)
    query_heads = heads_first(queries, key_value_count)
    grad_heads = heads_first(d_out, key_value_count)
    total_rows = rows * lax.axis_size("ctx")

    def scores_for(key_piece):
        key_heads = key_piece.reshape(key_piece.shape[0], key_value_count, HEAD_SIZE)
        return (
            jnp.einsum("kgtd,rkd->kgtr", query_heads, key_heads, preferred_element_type=jnp.float32)
            * scale
        )

    def forward_step(carry, key_piece, value_piece, start):
        allowed = key_mask(start, key_piece.shape[0], local_pattern, query_pos, span_order)

        def forward_update(state):
            running_max, total, weighted = state
            scores = scores_for(key_piece)
            new_max = jnp.maximum(running_max, jnp.max(jnp.where(allowed, scores, NEG), axis=-1))
            factor = jnp.exp(running_max - new_max)
            weights = jnp.where(allowed, jnp.exp(scores - new_max[..., None]), 0.0)
            value_heads = value_piece.reshape(
                value_piece.shape[0], key_value_count, HEAD_SIZE
            ).astype(jnp.float32)
            product = jnp.einsum(
                "kgtr,rkd->kgtd", weights, value_heads, precision=lax.Precision.HIGHEST
            )
            return (
                new_max,
                total * factor + jnp.sum(weights, axis=-1),
                weighted * factor[..., None] + product,
            )

        return lax.cond(jnp.any(allowed), forward_update, lambda state: state, carry)

    def make_backward(log_total, delta, anchor):

        def step(carry, key_piece, value_piece, start):
            count = key_piece.shape[0]
            allowed = key_mask(start, count, local_pattern, query_pos, span_order)

            def step_update(state):
                query_grad, key_grads = state
                key_heads = key_piece.reshape(count, key_value_count, HEAD_SIZE)
                value_heads = value_piece.reshape(count, key_value_count, HEAD_SIZE)
                scores = scores_for(key_piece)
                probs = jnp.where(allowed, jnp.exp(scores - log_total[..., None]), 0.0)
                grad_probs = jnp.einsum(
                    "kgtd,rkd->kgtr", grad_heads, value_heads, preferred_element_type=jnp.float32
                )
                grad_scores = (probs * (grad_probs - delta[..., None])).astype(jnp.bfloat16)
                query_grad = query_grad + jnp.einsum(
                    "kgtr,rkd->kgtd", grad_scores, key_heads, preferred_element_type=jnp.float32
                )
                key_part = (
                    jnp.einsum(
                        "kgtr,kgtd->rkd",
                        grad_scores,
                        query_heads,
                        preferred_element_type=jnp.float32,
                    )
                    * scale
                )
                value_part = jnp.einsum(
                    "kgtr,kgtd->rkd",
                    probs.astype(jnp.bfloat16),
                    grad_heads,
                    preferred_element_type=jnp.float32,
                )
                joined = jnp.stack(
                    (
                        key_part.reshape(count, key_value_count * HEAD_SIZE),
                        value_part.reshape(count, key_value_count * HEAD_SIZE),
                    ),
                    axis=1,
                )
                offset = start - anchor
                former = lax.dynamic_slice_in_dim(key_grads, offset, count, 0)
                key_grads = lax.dynamic_update_slice_in_dim(key_grads, former + joined, offset, 0)
                return (query_grad, key_grads)

            return lax.cond(jnp.any(allowed), step_update, lambda state: state, carry)

        return step

    start_state = (
        jnp.full((key_value_count, query_group, rows), NEG, jnp.float32),
        jnp.zeros((key_value_count, query_group, rows), jnp.float32),
        jnp.zeros((key_value_count, query_group, rows, HEAD_SIZE), jnp.float32),
    )
    query_zero = jnp.zeros((key_value_count, query_group, rows, HEAD_SIZE), jnp.float32)
    state = sweep(
        forward_step,
        start_state,
        lax.all_gather(keys, "ctx", axis=0, tiled=True),
        lax.all_gather(values, "ctx", axis=0, tiled=True),
        jnp.int32(0),
    )
    running_max, total, weighted = state
    attended = weighted / total[..., None]
    log_total = running_max + jnp.log(total)
    delta = jnp.sum(grad_heads * attended, axis=-1)
    log_total, delta = (log_total, delta)
    both_step = make_backward(log_total, delta, 0)
    grad_zero = jnp.zeros((total_rows, 2, key_value_count * HEAD_SIZE), jnp.float32)
    query_grad, key_grads = sweep(
        both_step,
        (query_zero, grad_zero),
        lax.all_gather(keys, "ctx", axis=0, tiled=True),
        lax.all_gather(values, "ctx", axis=0, tiled=True),
        jnp.int32(0),
    )
    summed = lax.psum_scatter(key_grads, "ctx", scatter_dimension=0, tiled=True)
    d_queries = (
        (query_grad * scale)
        .transpose(2, 0, 1, 3)
        .reshape(rows, key_value_count * query_group * HEAD_SIZE)
        .astype(jnp.bfloat16)
    )
    key_gradients = summed[:, 0, :].astype(jnp.bfloat16)
    value_gradients = summed[:, 1, :].astype(jnp.bfloat16)
    return (d_queries, key_gradients, value_gradients)


def on_device(queries, keys, values, d_out, span_order, pattern):
    count = lax.axis_size("ctx")
    if count == 4 and keys.shape[0] == BLOCK and pattern.shape == (count, 2):
        return routed(queries, keys, values, d_out, span_order, pattern)
    return swept(queries, keys, values, d_out, span_order, pattern)


def solution(mesh):
    return jax.shard_map(
        on_device,
        mesh=mesh,
        in_specs=(
            P(("grp", "ctx"), "head"),
            P(("grp", "ctx"), "head"),
            P(("grp", "ctx"), "head"),
            P(("grp", "ctx"), "head"),
            P(),
            P(),
        ),
        out_specs=(P(("grp", "ctx"), "head"), P(("grp", "ctx"), "head"), P(("grp", "ctx"), "head")),
        check_vma=False,
    )
```

```python
import functools
import itertools
import math

import jax
import jax.numpy as jnp
import numpy as np
from jax import lax
from jax.experimental import pallas as pl
from jax.experimental.pallas import tpu as pltpu
from jax.sharding import PartitionSpec as P

QUERY_HEADS = 64
KEY_VALUE_HEADS = 8
HEAD_SIZE = 128
BLOCK = 128


NEG = -1e30


PERMUTATIONS = {
    "a": (1, 2, 3, 0),
    "b": (1, 3, 0, 2),
    "c": (2, 0, 3, 1),
    "d": (3, 0, 1, 2),
    "e": (2, 3, 1, 0),
    "f": (3, 2, 0, 1),
    "s": (1, 0, 3, 2),
    "t": (2, 3, 0, 1),
    "u": (3, 2, 1, 0),
}
ROUTES = ("s", "b", "c", "a", "d", "e", "ab", "f", "ac", "bc", "bd", "ad", "dc", "ubc")


def route_tables():
    count = 4
    table = np.zeros(count**count, np.int32)
    sources = np.full((len(ROUTES), count - 1, count), -1, np.int32)
    targets = np.full((len(ROUTES), count - 1, count), -1, np.int32)
    pairs = []
    for k, route in enumerate(ROUTES):
        pairs.append(set())
        for r, name in enumerate(route):
            for source, target in enumerate(PERMUTATIONS[name]):
                if (source, target) not in pairs[k]:
                    sources[k, r, target], targets[k, r, source] = source, target
                    pairs[k].add((source, target))
    for shifts in itertools.product(range(count), repeat=count):
        need = {((i + shift) % count, i) for i, shift in enumerate(shifts) if shift}
        last = {i for i in range(count) if not shifts[i]}
        for _ in range(count):
            last |= {target for source, target in need if source in last}
        if len(last) == count:
            code = sum(shift * count**i for i, shift in enumerate(shifts))
            table[code] = next(k for k, held in enumerate(pairs) if need <= held)
    return np.concatenate((table, sources.ravel(), targets.ravel()))


def prepare_kernel(order_ref, pattern_ref, table_ref, keys_ref, values_ref, joined_ref, plan_ref):
    count = pattern_ref.shape[1]
    code = jnp.int32(0)
    for i in range(count):
        other = pattern_ref[1, i]
        shift = jnp.where(other < i, other - i + count, other - i)
        code += jnp.where(order_ref[other] < order_ref[i], shift, 0) * count**i
    route = table_ref[code]
    block = lax.axis_index("ctx")
    mine = pattern_ref[1, block]
    plan_ref[0] = route
    take = jnp.int32(0)
    for r in range(count - 1):
        place = count**count + (route * (count - 1) + r) * count + block
        take = jnp.where(table_ref[place] == mine, r, take)
        reader = table_ref[place + len(ROUTES) * (count - 1) * count]
        at = jnp.maximum(reader, 0)
        wanted = (reader >= 0) & (pattern_ref[1, at] == block)
        plan_ref[3 + r] = wanted.astype(jnp.int32)
    plan_ref[1] = take
    plan_ref[2] = (order_ref[mine] < order_ref[block]).astype(jnp.int32)
    width = keys_ref.shape[1]
    joined_ref[:, :width] = keys_ref[...]
    joined_ref[:, width:] = values_ref[...]


def span(start, size):
    if isinstance(start, int):
        return slice(start, start + size)
    return pl.ds(pl.multiple_of(start, size), size)


def columns_of(group, width, query_group):
    start = group * HEAD_SIZE
    heads = [span((group * query_group + head) * HEAD_SIZE, HEAD_SIZE) for head in range(query_group)]
    return span(start, HEAD_SIZE), span(width + start, HEAD_SIZE), heads


def stacked(ref, heads):
    return jnp.concatenate([ref[:, head] for head in heads], axis=0)


def against(rows, columns):
    return lax.dot_general(
        rows, columns, (((1,), (1,)), ((), ())), preferred_element_type=jnp.float32
    )


def picked(turn, choices):
    chosen = choices[0]
    for r in range(1, len(choices)):
        chosen = jnp.where(jnp.broadcast_to(turn[:, : chosen.shape[1]], chosen.shape) == r, choices[r], chosen)
    return chosen


LOG2_SCALE = math.log2(math.e) / math.sqrt(HEAD_SIZE)
SCALE = 1.0 / math.sqrt(HEAD_SIZE)


def own_kernel(
    query_group,
    plan_ref,
    queries_ref,
    grads_ref,
    own_ref,
    query_stack_ref,
    grad_stack_ref,
    weights_ref,
    d_probs_ref,
    stats_ref,
):
    rule = jnp.where(plan_ref[2] > 0, 0.0, jnp.full((1, stats_ref.shape[1]), NEG))
    turn = jnp.full((1, stats_ref.shape[1]), plan_ref[1].astype(jnp.float32))
    adds = [jnp.full((1, stats_ref.shape[1]), plan_ref[3 + r].astype(jnp.float32)) for r in range(3)]
    rows = queries_ref.shape[0]
    width = own_ref.shape[1] // 2
    shape = (rows, query_group * rows)
    allowed = lax.broadcasted_iota(jnp.int32, shape, 0) <= (
        lax.broadcasted_iota(jnp.int32, shape, 1) % rows
    )
    bias = jnp.where(allowed, 0.0, NEG)

    @pl.loop(0, width // HEAD_SIZE)
    def _(group):
        key_columns, value_columns, heads = columns_of(group, width, query_group)
        block = span(group * rows, rows)
        stack = span(group * query_group * rows, query_group * rows)
        query, grad = stacked(queries_ref, heads), stacked(grads_ref, heads)
        query_stack_ref[stack], grad_stack_ref[stack] = query, grad
        scores = against(own_ref[:, key_columns], query) * LOG2_SCALE + bias
        top = jnp.max(scores, axis=0, keepdims=True)
        weights = jnp.exp2(scores - top)
        d_probs = against(own_ref[:, value_columns], grad)
        weights_ref[block] = weights
        d_probs_ref[block] = d_probs
        total = jnp.sum(weights, axis=0, keepdims=True)
        delta = jnp.sum(weights * d_probs, axis=0, keepdims=True)
        stats_ref[span(group * 8, 8)] = jnp.concatenate((top, total, delta, rule, turn, *adds))


def other_kernel(
    query_group,
    unrolled,
    queries_ref,
    grads_ref,
    stats_ref,
    other_ref,
    sent_ref,
    d_scores_ref,
    joint_ref,
):
    rows, width = other_ref.shape[0], other_ref.shape[1] // 2
    groups = width // HEAD_SIZE

    def products(group):
        key_columns, value_columns, _ = columns_of(group, width, query_group)
        stack = span(group * query_group * rows, query_group * rows)
        return (
            against(other_ref[:, key_columns], queries_ref[stack]),
            against(other_ref[:, value_columns], grads_ref[stack]),
        )

    def step(group, scores, d_probs):
        key_columns, value_columns, _ = columns_of(group, width, query_group)
        stack = span(group * query_group * rows, query_group * rows)
        stats = stats_ref[span(group * 8, 8)]
        own_top, own_total, own_delta, bias = (stats[k : k + 1] for k in range(4))
        scores = scores * LOG2_SCALE + bias
        top = jnp.maximum(own_top, jnp.max(scores, axis=0, keepdims=True))
        factor = jnp.exp2(own_top - top)
        weights = jnp.exp2(scores - top)
        inverse = 1.0 / (own_total * factor + jnp.sum(weights, axis=0, keepdims=True))
        delta = (own_delta * factor + jnp.sum(weights * d_probs, axis=0, keepdims=True)) * inverse
        probs = weights * inverse
        d_scores = (probs * (d_probs - delta)).astype(jnp.bfloat16)
        d_scores_ref[span(group * rows, rows)] = d_scores
        blank = jnp.zeros((6, delta.shape[1]), jnp.float32)
        joint_ref[span(group * 8, 8)] = jnp.concatenate((factor * inverse, delta, blank))
        d_key = jnp.dot(d_scores, queries_ref[stack], preferred_element_type=jnp.float32) * SCALE
        d_value = jnp.dot(
            probs.astype(jnp.bfloat16), grads_ref[stack], preferred_element_type=jnp.float32
        )
        sent_ref[:, key_columns] = d_key.astype(jnp.bfloat16)
        sent_ref[:, value_columns] = d_value.astype(jnp.bfloat16)

    if unrolled:
        for group, made in enumerate([products(group) for group in range(groups)]):
            step(group, *made)
    else:
        pl.loop(0, groups)(lambda group: step(group, *products(group)))


def rest_kernel(
    query_group,
    rounds,
    queries_ref,
    grads_ref,
    stats_ref,
    own_ref,
    weights_ref,
    d_probs_ref,
    *refs,
):
    part_refs, d_scores_refs, joint_refs = (refs[k * rounds : (k + 1) * rounds] for k in range(3))
    d_queries_ref, d_keys_ref, d_values_ref = refs[3 * rounds :]
    rows, width = own_ref.shape[0], own_ref.shape[1] // 2

    @pl.loop(0, width // HEAD_SIZE)
    def _(group):
        key_columns, _, heads = columns_of(group, width, query_group)
        block = span(group * rows, rows)
        stack = span(group * query_group * rows, query_group * rows)
        query, grad = queries_ref[stack], grads_ref[stack]
        turn = stats_ref[span(group * 8, 8)][4:5]
        joint = picked(turn, [ref[span(group * 8, 8)] for ref in joint_refs])
        probs = weights_ref[block] * joint[:1]
        d_scores = (probs * (d_probs_ref[block] - joint[1:2])).astype(jnp.bfloat16)
        d_key = jnp.dot(d_scores, query, preferred_element_type=jnp.float32) * SCALE
        d_value = jnp.dot(probs.astype(jnp.bfloat16), grad, preferred_element_type=jnp.float32)
        d_keys_ref[:, key_columns] = d_key
        d_values_ref[:, key_columns] = d_value
        other_key = picked(turn, [ref[:, key_columns] for ref in part_refs])
        both = jnp.concatenate((d_scores, picked(turn, [ref[block] for ref in d_scores_refs])), axis=0)
        key = jnp.concatenate((own_ref[:, key_columns], other_key), axis=0)
        d_query = lax.dot_general(
            both, key, (((0,), (0,)), ((), ())), preferred_element_type=jnp.float32
        )
        d_query = (d_query * SCALE).astype(jnp.bfloat16)
        for index, head in enumerate(heads):
            d_queries_ref[:, head] = d_query[index * rows : (index + 1) * rows]


def routed(queries, keys, values, d_out, span_order, pattern):
    rows, width = keys.shape
    count = pattern.shape[0]
    query_group = QUERY_HEADS // KEY_VALUE_HEADS
    groups = width // HEAD_SIZE
    smem = pl.BlockSpec(memory_space=pltpu.SMEM)
    vmem = pl.BlockSpec(memory_space=pltpu.VMEM)

    def shaped(shape, dtype):
        return jax.ShapeDtypeStruct(shape, dtype)

    def kernel(name, body, results, inputs):
        products = 2 * groups * query_group * rows * rows * HEAD_SIZE
        return pl.pallas_call(
            functools.partial(body, query_group),
            out_shape=results,
            in_specs=[vmem if x.ndim == 2 else smem for x in inputs],
            out_specs=tuple(vmem for _ in results),
            compiler_params=pltpu.CompilerParams(vmem_limit_bytes=16 << 20),
            cost_estimate=pl.CostEstimate(
                flops=4 * products,
                bytes_accessed=sum(x.size * x.dtype.itemsize for x in (*inputs, *results)),
                transcendentals=groups * query_group * rows * rows,
            ),
            name=name,
        )(*inputs)

    wide = (groups * rows, query_group * rows)
    narrow = (groups * 8, query_group * rows)
    stack = shaped((groups * query_group * rows, HEAD_SIZE), jnp.bfloat16)
    joined, plan = pl.pallas_call(
        prepare_kernel,
        out_shape=(shaped((rows, 2 * width), jnp.bfloat16), shaped((count + 2,), jnp.int32)),
        in_specs=[smem, smem, smem, vmem, vmem],
        out_specs=(vmem, smem),
        name="prepare",
    )(span_order, pattern.T, jnp.asarray(route_tables()), keys, values)

    def along(route):
        rounds = [list(enumerate(PERMUTATIONS[name])) for name in route]

        def branch(plan, queries, d_out, joined):
            parts = [lax.ppermute(joined, "ctx", pairs) for pairs in rounds]
            query_stack, grad_stack, weights, d_probs, stats = kernel(
                "own_block",
                own_kernel,
                (
                    stack,
                    stack,
                    shaped(wide, jnp.float32),
                    shaped(wide, jnp.float32),
                    shaped(narrow, jnp.float32),
                ),
                (plan, queries, d_out, joined),
            )
            returned, d_scores, joints = [], [], []
            for part, pairs in zip(parts, rounds):
                sent, d_score, joint = kernel(
                    "other_block",
                    lambda query_group, *refs: other_kernel(query_group, len(rounds) == 1, *refs),
                    (
                        shaped((rows, 2 * width), jnp.bfloat16),
                        shaped(wide, jnp.bfloat16),
                        shaped(narrow, jnp.float32),
                    ),
                    (query_stack, grad_stack, stats, part),
                )
                back = [(target, source) for source, target in pairs]
                returned.append(lax.ppermute(sent, "ctx", back))
                d_scores.append(d_score)
                joints.append(joint)
            own = (query_stack, grad_stack, stats, joined, weights, d_probs)
            d_queries, d_keys, d_values = kernel(
                "rest",
                lambda query_group, *refs: rest_kernel(query_group, len(rounds), *refs),
                (
                    shaped(queries.shape, jnp.bfloat16),
                    shaped((rows, width), jnp.float32),
                    shaped((rows, width), jnp.float32),
                ),
                (*own, *parts, *d_scores, *joints),
            )
            for r, terms in enumerate(returned):
                terms = terms.astype(jnp.float32)
                if len(returned) > 1:
                    terms = jnp.where(stats[5 + r : 6 + r, : 2 * width] > 0.0, terms, 0.0)
                d_keys, d_values = d_keys + terms[:, :width], d_values + terms[:, width:]
            return d_queries, d_keys.astype(jnp.bfloat16), d_values.astype(jnp.bfloat16)

        return branch

    return lax.switch(plan[0], [along(route) for route in ROUTES], plan, queries, d_out, joined)


def heads_first(dense_matrix, key_value_count):
    return dense_matrix.reshape(
        dense_matrix.shape[0], key_value_count, QUERY_HEADS // KEY_VALUE_HEADS, HEAD_SIZE
    ).transpose(1, 2, 0, 3)


def key_mask(start, count, local_pattern, query_pos, span_order):
    key_blocks = start // BLOCK + jnp.arange(count // BLOCK, dtype=jnp.int32)
    named = jnp.any(local_pattern[:, :, None] == key_blocks[None, None, :], axis=1)
    local_blocks = local_pattern.shape[0]
    named_rows = jnp.broadcast_to(
        named[:, None, :, None], (local_blocks, BLOCK, count // BLOCK, BLOCK)
    )
    named_rows = named_rows.reshape(local_blocks * BLOCK, count)
    key_order = lax.dynamic_slice_in_dim(span_order, start // BLOCK, count // BLOCK, 0)
    key_pos = (key_order[:, None] * BLOCK + jnp.arange(BLOCK, dtype=jnp.int32)[None, :]).reshape(
        count
    )
    return named_rows & (key_pos[None, :] <= query_pos[:, None])


def sweep(step, carry, key_piece, value_piece, start):
    count = key_piece.shape[0]
    width = BLOCK * math.gcd(count // BLOCK, max(1, 512 // BLOCK))
    turns = count // width
    if turns == 1:
        return step(carry, key_piece, value_piece, start)

    def advance(index, inner):
        offset = index * width
        key_part = lax.dynamic_slice_in_dim(key_piece, offset, width, 0)
        value_part = lax.dynamic_slice_in_dim(value_piece, offset, width, 0)
        return step(inner, key_part, value_part, start + offset)

    return lax.fori_loop(0, turns, advance, carry)


def swept(queries, keys, values, d_out, span_order, pattern):
    rows = queries.shape[0]
    key_value_count = keys.shape[1] // HEAD_SIZE
    query_group = QUERY_HEADS // KEY_VALUE_HEADS
    blocks_here = rows // BLOCK
    scale = 1.0 / math.sqrt(HEAD_SIZE)
    first_block = lax.axis_index("ctx") * blocks_here
    local_pattern = lax.dynamic_slice_in_dim(pattern, first_block, blocks_here, 0)
    local_order = lax.dynamic_slice_in_dim(span_order, first_block, blocks_here, 0)
    query_pos = (
        local_order[:, None] * BLOCK + jnp.arange(BLOCK, dtype=jnp.int32)[None, :]
    ).reshape(rows)
    query_heads = heads_first(queries, key_value_count)
    grad_heads = heads_first(d_out, key_value_count)
    total_rows = rows * lax.axis_size("ctx")

    def scores_for(key_piece):
        key_heads = key_piece.reshape(key_piece.shape[0], key_value_count, HEAD_SIZE)
        return (
            jnp.einsum("kgtd,rkd->kgtr", query_heads, key_heads, preferred_element_type=jnp.float32)
            * scale
        )

    def forward_step(carry, key_piece, value_piece, start):
        allowed = key_mask(start, key_piece.shape[0], local_pattern, query_pos, span_order)

        def forward_update(state):
            running_max, total, weighted = state
            scores = scores_for(key_piece)
            new_max = jnp.maximum(running_max, jnp.max(jnp.where(allowed, scores, NEG), axis=-1))
            factor = jnp.exp(running_max - new_max)
            weights = jnp.where(allowed, jnp.exp(scores - new_max[..., None]), 0.0)
            value_heads = value_piece.reshape(
                value_piece.shape[0], key_value_count, HEAD_SIZE
            ).astype(jnp.float32)
            product = jnp.einsum(
                "kgtr,rkd->kgtd", weights, value_heads, precision=lax.Precision.HIGHEST
            )
            return (
                new_max,
                total * factor + jnp.sum(weights, axis=-1),
                weighted * factor[..., None] + product,
            )

        return lax.cond(jnp.any(allowed), forward_update, lambda state: state, carry)

    def make_backward(log_total, delta, anchor):

        def step(carry, key_piece, value_piece, start):
            count = key_piece.shape[0]
            allowed = key_mask(start, count, local_pattern, query_pos, span_order)

            def step_update(state):
                query_grad, key_grads = state
                key_heads = key_piece.reshape(count, key_value_count, HEAD_SIZE)
                value_heads = value_piece.reshape(count, key_value_count, HEAD_SIZE)
                scores = scores_for(key_piece)
                probs = jnp.where(allowed, jnp.exp(scores - log_total[..., None]), 0.0)
                grad_probs = jnp.einsum(
                    "kgtd,rkd->kgtr", grad_heads, value_heads, preferred_element_type=jnp.float32
                )
                grad_scores = (probs * (grad_probs - delta[..., None])).astype(jnp.bfloat16)
                query_grad = query_grad + jnp.einsum(
                    "kgtr,rkd->kgtd", grad_scores, key_heads, preferred_element_type=jnp.float32
                )
                key_part = (
                    jnp.einsum(
                        "kgtr,kgtd->rkd",
                        grad_scores,
                        query_heads,
                        preferred_element_type=jnp.float32,
                    )
                    * scale
                )
                value_part = jnp.einsum(
                    "kgtr,kgtd->rkd",
                    probs.astype(jnp.bfloat16),
                    grad_heads,
                    preferred_element_type=jnp.float32,
                )
                joined = jnp.stack(
                    (
                        key_part.reshape(count, key_value_count * HEAD_SIZE),
                        value_part.reshape(count, key_value_count * HEAD_SIZE),
                    ),
                    axis=1,
                )
                offset = start - anchor
                former = lax.dynamic_slice_in_dim(key_grads, offset, count, 0)
                key_grads = lax.dynamic_update_slice_in_dim(key_grads, former + joined, offset, 0)
                return (query_grad, key_grads)

            return lax.cond(jnp.any(allowed), step_update, lambda state: state, carry)

        return step

    start_state = (
        jnp.full((key_value_count, query_group, rows), NEG, jnp.float32),
        jnp.zeros((key_value_count, query_group, rows), jnp.float32),
        jnp.zeros((key_value_count, query_group, rows, HEAD_SIZE), jnp.float32),
    )
    query_zero = jnp.zeros((key_value_count, query_group, rows, HEAD_SIZE), jnp.float32)
    state = sweep(
        forward_step,
        start_state,
        lax.all_gather(keys, "ctx", axis=0, tiled=True),
        lax.all_gather(values, "ctx", axis=0, tiled=True),
        jnp.int32(0),
    )
    running_max, total, weighted = state
    attended = weighted / total[..., None]
    log_total = running_max + jnp.log(total)
    delta = jnp.sum(grad_heads * attended, axis=-1)
    log_total, delta = (log_total, delta)
    both_step = make_backward(log_total, delta, 0)
    grad_zero = jnp.zeros((total_rows, 2, key_value_count * HEAD_SIZE), jnp.float32)
    query_grad, key_grads = sweep(
        both_step,
        (query_zero, grad_zero),
        lax.all_gather(keys, "ctx", axis=0, tiled=True),
        lax.all_gather(values, "ctx", axis=0, tiled=True),
        jnp.int32(0),
    )
    summed = lax.psum_scatter(key_grads, "ctx", scatter_dimension=0, tiled=True)
    d_queries = (
        (query_grad * scale)
        .transpose(2, 0, 1, 3)
        .reshape(rows, key_value_count * query_group * HEAD_SIZE)
        .astype(jnp.bfloat16)
    )
    key_gradients = summed[:, 0, :].astype(jnp.bfloat16)
    value_gradients = summed[:, 1, :].astype(jnp.bfloat16)
    return (d_queries, key_gradients, value_gradients)


def on_device(queries, keys, values, d_out, span_order, pattern):
    count = lax.axis_size("ctx")
    if count == 4 and keys.shape[0] == BLOCK and pattern.shape == (count, 2):
        return routed(queries, keys, values, d_out, span_order, pattern)
    return swept(queries, keys, values, d_out, span_order, pattern)


def solution(mesh):
    return jax.shard_map(
        on_device,
        mesh=mesh,
        in_specs=(
            P(("grp", "ctx"), "head"),
            P(("grp", "ctx"), "head"),
            P(("grp", "ctx"), "head"),
            P(("grp", "ctx"), "head"),
            P(),
            P(),
        ),
        out_specs=(P(("grp", "ctx"), "head"), P(("grp", "ctx"), "head"), P(("grp", "ctx"), "head")),
        check_vma=False,
    )
```
